32 devices in a mesh: seq: 8 (over z, x), head: 4 (over y, core).
Axes of the slice: x: 2, y: 2, z: 4, core: 2. Of those that a mesh axis runs over, the one named last changes fastest.
Arguments:
- query_rows: bfloat16 [6144, 4096], P('seq', 'head'), may hold values from -6 to 6
- key_rows: bfloat16 [6144, 4096], P('seq', 'head'), may hold values from -6 to 6
- value_rows: bfloat16 [6144, 4096], P('seq', 'head'), may hold values from -6 to 6
- grad_out: bfloat16 [6144, 4096], P('seq', 'head'), may hold values from -6 to 6
- doc_lengths: int32 [16], replicated, may hold values from 1 to 4224, as said below
Outputs:
- attended: bfloat16 [6144, 4096], P('seq', 'head')
- grad_query: bfloat16 [6144, 4096], P('seq', 'head')
- grad_key: bfloat16 [6144, 4096], P('seq', 'head')
- grad_value: bfloat16 [6144, 4096], P('seq', 'head')
The draws below stay inside these ranges and needn't reach their ends.
Inputs may be any that keep to these rules, and one draw needn't show every extreme that they name: `doc_lengths`: the 16 lengths sum to 6144; the last document is the longest, exactly 4224 long, and the first is longer than 768.
All inputs are finite; a program needn't handle non-finite values.
Results may differ from the reference program's by a relative error of at most 0.0043.
Values sent between devices are 32-bit elements; how exact they have to be, the bound alone decides.
No kernel may reach another device: no remote copies, remote signals or barrier semaphores. Data moves between devices by JAX's collectives and lax.ppermute only.
A program may use at most 128 MiB of HBM per device.

```python
import jax
import jax.numpy as jnp
from jax import lax

DH = 128
HEADS = 32
T_DEV = 768
DOCS = 16
TOKENS = 6144
DOC_MOST = 4224


def draw_doc_lengths(key, part):
    rest = TOKENS - DOC_MOST
    pool = jnp.arange(T_DEV + 1, rest, dtype=jnp.int32)
    picks = jax.random.permutation(jax.random.fold_in(key, 11), pool)[:DOCS - 2]
    cuts = jnp.sort(picks)
    edges = jnp.concatenate([jnp.zeros((1,), jnp.int32), cuts, jnp.full((1,), rest, jnp.int32)])
    lengths = edges[1:] - edges[:-1]
    return jnp.concatenate([lengths, jnp.full((1,), DOC_MOST, jnp.int32)]).astype(jnp.int32)


def block_scale(key, extent, cuts, low, high):
    loudness = 1.0
    for position, shards_of in cuts:
        steps = jax.random.uniform(jax.random.fold_in(jax.random.fold_in(key, 6), position), (shards_of,), jnp.float32, low / len(cuts), high / len(cuts))
        loudness = loudness * jnp.repeat(jnp.exp(steps), extent[position] // shards_of).reshape((-1,) + (1,) * (len(extent) - 1 - position))
    return loudness


def bell_draw(key, shape, width, reach, cuts=(), kind=jnp.bfloat16):
    entries = width * jax.random.normal(key, shape, jnp.float32)
    if cuts:
        entries = entries * block_scale(key, shape, cuts, -0.22, 0.18)
    return jnp.clip(entries, -reach, reach).astype(kind)


def setup_inputs(seed: int = 0) -> dict:
    streams_of = jax.random.split(jax.random.key(seed), 6)
    return {
        "query_rows": bell_draw(streams_of[0], (TOKENS, HEADS * DH), 1.0, 6.0, ((0, 8), (1, 4))),
        "key_rows": bell_draw(streams_of[1], (TOKENS, HEADS * DH), 1.0, 6.0, ((0, 8), (1, 4))),
        "value_rows": bell_draw(streams_of[2], (TOKENS, HEADS * DH), 1.0, 6.0, ((0, 8), (1, 4))),
        "grad_out": bell_draw(streams_of[3], (TOKENS, HEADS * DH), 1.0, 6.0, ((0, 8), (1, 4))),
        "doc_lengths": draw_doc_lengths(jax.random.fold_in(streams_of[5], 71), 0),
    }


def doc_layout(doc_lengths, offset, count):
    starts = jnp.cumsum(doc_lengths, dtype=jnp.int32) - doc_lengths
    positions = offset + jnp.arange(count, dtype=jnp.int32)
    first_start = lax.optimization_barrier(jnp.max(jnp.where(starts[None, :] <= positions[:, None], starts[None, :], 0), axis=1))
    counts = (positions - first_start + 1).astype(jnp.float32)
    rowscale = 1.0 / jnp.sqrt(counts * DH)
    order = jnp.arange(count, dtype=jnp.int32)
    same_doc = (first_start[:, None] == first_start[None, :]) & (order[None, :] <= order[:, None])
    head_mask = (first_start < offset).astype(jnp.float32)
    tail_mask = (first_start == first_start[count - 1]).astype(jnp.float32)
    has_start = (first_start[count - 1] >= offset).astype(jnp.float32).reshape(1)
    return (rowscale, same_doc, head_mask, tail_mask, has_start)

def to_low(values):
    return lax.optimization_barrier(values.astype(jnp.bfloat16)).astype(jnp.float32)

def block_parts(block, query_blk, key_blk, value_blk, grad_blk, doc_lengths, block_size):
    highest = lax.Precision.HIGHEST
    offset = block * block_size
    rowscale, same_doc, head_mask, tail_mask, has_start = doc_layout(doc_lengths, offset, block_size)
    query_f = query_blk.astype(jnp.float32)
    key_f = key_blk.astype(jnp.float32)
    value_f = value_blk.astype(jnp.float32)
    grad_f = grad_blk.astype(jnp.float32)
    scores = jnp.where(same_doc[None], jnp.einsum('thd,shd->hts', query_f, key_f, precision=highest), 0.0)
    raw_grad = jnp.einsum('thd,shd->hts', grad_f, value_f, precision=highest)
    grad_scores = jnp.where(same_doc[None], raw_grad * rowscale[None, :, None], 0.0)
    scaled = rowscale[:, None, None] * grad_f
    return (rowscale, head_mask, tail_mask, has_start, query_f, key_f, value_f, to_low(scores), to_low(grad_scores), scaled, to_low(scaled))

def reference(query_rows, key_rows, value_rows, grad_out, doc_lengths):
    highest = lax.Precision.HIGHEST
    block_size = T_DEV
    block_count = TOKENS // block_size
    shape4 = (block_count, block_size, HEADS, DH)
    blocks = (jnp.arange(block_count, dtype=jnp.int32), query_rows.reshape(shape4), key_rows.reshape(shape4), value_rows.reshape(shape4), grad_out.reshape(shape4))

    def forward_step(state_in, inputs):
        block, query_blk, key_blk, value_blk, grad_blk = inputs
        rowscale, head_mask, tail_mask, has_start, query_f, key_f, value_f, scores_low, grad_low, scaled, scaled_low = block_parts(block, query_blk, key_blk, value_blk, grad_blk, doc_lengths, block_size)
        carried = jnp.einsum('thi,hij->thj', query_f, state_in, precision=highest)
        attended = rowscale[:, None, None] * (jnp.einsum('hts,shd->thd', scores_low, value_f, precision=highest) + head_mask[:, None, None] * carried)
        grad_query = jnp.einsum('hts,shd->thd', grad_low, key_f, precision=highest) + head_mask[:, None, None] * jnp.einsum('hij,thj->thi', state_in, scaled, precision=highest)
        tail_keys = key_f * tail_mask[:, None, None]
        state_out = jnp.where(has_start > 0.5, 0.0, state_in) + jnp.einsum('shi,shj->hij', tail_keys, value_f, precision=highest)
        return (state_out, (attended.astype(jnp.bfloat16), grad_query.astype(jnp.bfloat16)))

    def backward_step(grad_in, inputs):
        block, query_blk, key_blk, value_blk, grad_blk = inputs
        rowscale, head_mask, tail_mask, has_start, query_f, key_f, value_f, scores_low, grad_low, scaled, scaled_low = block_parts(block, query_blk, key_blk, value_blk, grad_blk, doc_lengths, block_size)
        grad_key = jnp.einsum('hts,thd->shd', grad_low, query_f, precision=highest) + tail_mask[:, None, None] * jnp.einsum('hij,shj->shi', grad_in, value_f, precision=highest)
        grad_value = jnp.einsum('hts,thd->shd', scores_low, scaled_low, precision=highest) + tail_mask[:, None, None] * jnp.einsum('shi,hij->shj', key_f, grad_in, precision=highest)
        head_queries = query_f * head_mask[:, None, None]
        grad_next = jnp.where(has_start > 0.5, 0.0, grad_in) + jnp.einsum('thi,thj->hij', head_queries, scaled, precision=highest)
        return (grad_next, (grad_key.astype(jnp.bfloat16), grad_value.astype(jnp.bfloat16)))
    zero_state = jnp.zeros((HEADS, DH, DH), jnp.float32)
    _, (attended, grad_query) = lax.scan(forward_step, zero_state, blocks)
    _, (grad_key, grad_value) = lax.scan(backward_step, zero_state, blocks, reverse=True)
    flat = (TOKENS, HEADS * DH)
    return (attended.reshape(flat), grad_query.reshape(flat), grad_key.reshape(flat), grad_value.reshape(flat))
```

```python
import functools

import jax
import jax.numpy as jnp
from jax import lax
from jax.experimental import pallas as pl
from jax.experimental.pallas import tpu as pltpu
from jax.sharding import PartitionSpec as P

DH = 128
ROWS = 256
F32 = jnp.float32
LOW = jnp.bfloat16

NT = (((1,), (1,)), ((), ()))
TN = (((0,), (0,)), ((), ()))
NN = (((1,), (0,)), ((), ()))


def dot(a, b, dims):
    return lax.dot_general(a, b, dims, preferred_element_type=F32)


def split(a):
    high = a.astype(LOW)
    return high, (a - high.astype(F32)).astype(LOW)


def layout_columns(lengths, offset, count):
    row = lax.broadcasted_iota(jnp.int32, (count, DH), 0) + offset
    first = jnp.zeros((count, DH), jnp.int32)
    start = jnp.int32(0)
    for j in range(lengths.shape[0]):
        first = jnp.where(row >= start, start, first)
        start = start + lengths[j]
    scale = 1.0 / jnp.sqrt((row - first + 1).astype(F32) * DH)
    return scale, first - offset


def state_kernel(make_layout, lengths, q_ref, k_ref, v_ref, g_ref, *refs):
    count = q_ref.shape[0]
    if make_layout:
        kv_ref, qg_ref, scale_ref, first_ref = refs

        @pl.when(pl.program_id(0) == 0)
        def _():
            scale, first = layout_columns(lengths, lax.axis_index("seq") * count, count)
            scale_ref[...] = scale
            first_ref[...] = first
    else:
        scale_ref, first_ref, kv_ref, qg_ref = refs
    first = first_ref[...]
    row = lax.broadcasted_iota(jnp.int32, (count, DH), 0)
    tail_start = first_ref[count - 1, 0]
    for h in range(kv_ref.shape[0]):
        cols = slice(h * DH, (h + 1) * DH)
        tail = jnp.where(row >= tail_start, k_ref[:, cols], jnp.zeros((), LOW))
        kv_ref[h] = dot(tail, v_ref[:, cols], TN)
        scaled = jnp.where(first < 0, scale_ref[...] * g_ref[:, cols].astype(F32), 0.0)
        high, rest = split(scaled)
        both = dot(q_ref[:, cols], jnp.concatenate([high, rest], axis=1), TN)
        qg_ref[h] = both[:, :DH] + both[:, DH:]


def local_kernel(q_ref, k_ref, v_ref, g_ref, scale_ref, first_ref, a_ref, dq_ref, dk_ref, dv_ref):
    count = q_ref.shape[0]
    for r in range(0, count, ROWS):
        rows = slice(r, r + ROWS)
        wide = r + ROWS
        q, g = q_ref[rows], g_ref[rows]
        k, v = k_ref[:wide], v_ref[:wide]
        scale = scale_ref[rows]
        many = wide // DH
        first_w = jnp.concatenate([first_ref[rows]] * many, axis=1)
        scale_w = jnp.concatenate([scale] * many, axis=1)
        row = lax.broadcasted_iota(jnp.int32, (ROWS, wide), 0) + r
        col = lax.broadcasted_iota(jnp.int32, (ROWS, wide), 1)
        mask = (col >= first_w) & (col <= row)
        scores = jnp.where(mask, dot(q, k, NT), 0.0).astype(LOW)
        grads = jnp.where(mask, dot(g, v, NT) * scale_w, 0.0).astype(LOW)
        scaled = (scale * g.astype(F32)).astype(LOW)
        a_ref[rows] = scale * dot(scores, v, NN)
        dq_ref[rows] = dot(grads, k, NN)
        dk = dot(grads, q, TN)
        dv = dot(scores, scaled, TN)
        if r:
            dk_ref[:r] += dk[:r]
            dv_ref[:r] += dv[:r]
        dk_ref[rows] = dk[r:]
        dv_ref[rows] = dv[r:]


def final_kernel(
    q_ref, k_ref, v_ref, g_ref, a_ref, dq_ref, dk_ref, dv_ref, kv_ref, qg_ref, scale_ref, first_ref, *refs
):
    out_a, out_q, out_k, out_v = refs[-4:]
    count = q_ref.shape[0]
    scale = jnp.where(first_ref[...] < 0, scale_ref[...], 0.0)
    row = lax.broadcasted_iota(jnp.int32, (count, DH), 0)
    tail = row >= first_ref[count - 1, 0]

    def carried(rows_ref, state, dims):
        high, rest = split(state)
        rows = rows_ref[...]
        return dot(rows, high, dims) + dot(rows, rest, dims)

    kv = kv_ref[0]
    qg = qg_ref[0]
    out_a[...] = (a_ref[...] + scale * carried(q_ref, kv, NN)).astype(LOW)
    out_q[...] = (dq_ref[...] + scale * carried(g_ref, kv, NT)).astype(LOW)
    out_k[...] = (dk_ref[...] + jnp.where(tail, carried(v_ref, qg, NT), 0.0)).astype(LOW)
    out_v[...] = (dv_ref[...] + jnp.where(tail, carried(k_ref, qg, NN), 0.0)).astype(LOW)


def head_block(count, base=0):
    return pl.BlockSpec((count, DH), lambda i, *_: (0, base + i))


def whole(count):
    return pl.BlockSpec((count, DH), lambda i, *_: (0, 0))


STATE = pl.BlockSpec((1, DH, DH), lambda i, *_: (i, 0, 0))


def states(arrays, lengths, base, heads, layout):
    count = arrays[0].shape[0]
    shape = jax.ShapeDtypeStruct((heads, DH, DH), F32)
    out_shape = [shape, shape]
    out_specs = [STATE, STATE]
    in_specs = [head_block(count, base)] * 4
    if layout is None:
        out_shape += [jax.ShapeDtypeStruct((count, DH), F32), jax.ShapeDtypeStruct((count, DH), jnp.int32)]
        out_specs += [whole(count)] * 2
    else:
        in_specs += [whole(count)] * 2
    return pl.pallas_call(
        functools.partial(state_kernel, layout is None),
        out_shape=out_shape,
        grid_spec=pltpu.PrefetchScalarGridSpec(
            num_scalar_prefetch=1, grid=(heads,), in_specs=in_specs, out_specs=out_specs
        ),
        name="states",
    )(lengths, *arrays, *(layout or ()))


def local(arrays, layout, base, heads):
    count = arrays[0].shape[0]
    shape = jax.ShapeDtypeStruct((count, heads * DH), F32)
    return pl.pallas_call(
        local_kernel,
        out_shape=[shape] * 4,
        grid=(heads,),
        in_specs=[head_block(count, base)] * 4 + [whole(count)] * 2,
        out_specs=[head_block(count)] * 4,
        name="local",
    )(*arrays, *layout)


def final(arrays, parts, kv, qg, layout, base, outs):
    count, width = arrays[0].shape
    heads = kv.shape[0]
    shape = jax.ShapeDtypeStruct((count, width), LOW)
    extra = tuple(outs or ())
    return pl.pallas_call(
        final_kernel,
        out_shape=[shape] * 4,
        grid=(heads,),
        in_specs=[head_block(count, base)] * 4
        + [head_block(count)] * 4
        + [STATE] * 2
        + [whole(count)] * 2
        + [pl.BlockSpec(memory_space=pl.ANY)] * len(extra),
        out_specs=[head_block(count, base)] * 4,
        input_output_aliases={12 + i: i for i in range(len(extra))},
        name="final",
    )(*arrays, *parts, kv, qg, *layout, *extra)


PAIRS = [(d, d ^ 1) for d in range(8)]
UP_1 = [(0, 2), (2, 4), (3, 5)]
UP_2 = [(0, 2), (4, 6), (5, 7)]
DOWN_1 = [(2, 0), (6, 4), (7, 5)]
DOWN_2 = [(2, 0), (4, 2), (5, 3)]


def choose(place, default, *cases):
    value = default
    for devices, other in cases:
        hit = functools.reduce(jnp.logical_or, [place == d for d in devices])
        value = jnp.where(hit, other, value)
    return value


class Exchange:
    def __init__(self, kv, qg, place, joined):
        half = kv.shape[0] // 2
        self.half, self.place, self.joined = half, place, joined
        self.k = (kv[:half], kv[half:])
        self.q = (qg[:half], qg[half:])
        self.odd = place % 2 == 1
        self.mine_k = jnp.where(self.odd, self.k[1], self.k[0])
        self.mine_q = jnp.where(self.odd, self.q[1], self.q[0])
        self.give_k = jnp.where(self.odd, self.k[0], self.k[1])
        self.give_q = jnp.where(self.odd, self.q[0], self.q[1])

    def swap(self, value):
        return lax.ppermute(value, "seq", PAIRS)

    def step0(self):
        send = choose(self.place, self.give_k, ((0, 1), self.k[0]), ((6, 7), self.give_q))
        self.x0 = self.swap(send)

    def step1(self):
        d = self.place
        self.sum_k = self.mine_k + self.x0
        self.sum_q6 = self.mine_q + self.x0
        link = jnp.where(self.joined, 1.0, 0.0)
        send = choose(
            d, self.give_q, ((0, 1), self.k[1]), ((2,), self.k[0]), ((3,), self.q[0]), ((6,), self.k[1]), ((7,), self.q[1])
        )
        up = choose(d, self.sum_k, ((0,), self.x0 + link * self.k[0]))
        down = choose(d, self.sum_q6, ((2,), self.q[0]))
        self.x1 = self.swap(send)
        self.up1 = lax.ppermute(up, "seq", UP_1)
        self.down1 = lax.ppermute(down, "seq", DOWN_1)

    def step2(self):
        d = self.place
        link = jnp.where(self.joined, 1.0, 0.0)
        self.sum_q = self.mine_q + self.x1
        up = choose(d, self.up1 + self.sum_k, ((0,), self.x1 + link * self.k[1]))
        down = choose(d, self.down1 + self.sum_q, ((2,), self.q[1]))
        send = choose(d, self.up1, ((0,), self.down1), ((1,), self.q[0]), ((4,), self.up1 + self.k[0]))
        self.x2 = self.swap(send)
        self.up2 = lax.ppermute(up, "seq", UP_2)
        self.down2 = lax.ppermute(down, "seq", DOWN_2)

    def step3(self):
        d = self.place
        send = choose(
            d,
            self.down1,
            ((0, 2), self.down2),
            ((1,), self.q[1]),
            ((3,), self.down2 + self.q[1]),
            ((5,), self.down1 + self.q[1]),
            ((6,), self.up2 + self.k[0]),
            ((7,), self.up2),
        )
        self.x3 = self.swap(send)

    def result(self):
        d = self.place
        link = jnp.where(self.joined, 1.0, 0.0)
        zero = jnp.zeros_like(self.x0)
        kv_low = choose(
            d,
            zero,
            ((1,), self.x0),
            ((2, 4), self.up1),
            ((3,), self.x1),
            ((5,), self.x2),
            ((6,), self.up2),
            ((7,), self.x3),
        )
        kv_high = choose(
            d,
            zero,
            ((1,), self.x1),
            ((2,), self.up2),
            ((3,), self.x0),
            ((4,), self.x2),
            ((5,), self.up1 + self.x0),
            ((6,), self.x3),
            ((7,), self.up2 + self.x1),
        )
        qg_low = choose(
            d,
            zero,
            ((0,), self.x2 + link * self.down1),
            ((1,), self.x2),
            ((2,), self.x1 + self.down2),
            ((3,), self.x3),
            ((4,), self.x1 + self.down1),
            ((5,), self.x3),
            ((6,), self.x0),
        )
        qg_high = choose(
            d,
            zero,
            ((0,), self.x3 + link * self.down2),
            ((1,), self.x3),
            ((2,), self.x3),
            ((3,), self.down2),
            ((4,), self.x3),
            ((5,), self.down1),
            ((6,), self.x1),
        )
        return jnp.concatenate([kv_low, kv_high]), jnp.concatenate([qg_low, qg_high])


def gathered_states(kv, qg, starts_here):
    count = lax.axis_size("seq")
    place = lax.axis_index("seq")
    kv_all, qg_all, start_all = lax.all_gather((kv, qg, starts_here), "seq")
    order = jnp.arange(count)
    last_start = jnp.max(jnp.where((order < place) & (start_all > 0.5), order, 0))
    next_start = jnp.min(jnp.where((order > place) & (start_all > 0.5), order, count))
    before = (order < place) & (order >= last_start)
    after = (order > place) & (order <= next_start)

    def total(pick, values):
        return jnp.sum(jnp.where(pick[:, None, None, None], values, 0.0), axis=0)

    return total(before, kv_all), total(after, qg_all)


def per_device(query_rows, key_rows, value_rows, grad_out, doc_lengths):
    arrays = (query_rows, key_rows, value_rows, grad_out)
    count, width = query_rows.shape
    heads = width // DH
    place = lax.axis_index("seq")
    if lax.axis_size("seq") != 8:
        kv, qg, *layout = states(arrays, doc_lengths, 0, heads, None)
        starts_here = (layout[1][count - 1, 0] >= 0).astype(F32)
        parts = local(arrays, layout, 0, heads)
        kv, qg = gathered_states(kv, qg, starts_here)
        return tuple(final(arrays, parts, kv, qg, layout, 0, None))
    joined = doc_lengths[0] >= 2 * count
    chunks = 2
    each = heads // chunks
    kv, qg, *layout = states(arrays, doc_lengths, 0, each, None)
    flows = [Exchange(kv, qg, place, joined)]
    for c in range(1, chunks):
        kv, qg = states(arrays, doc_lengths, c * each, each, layout)
        flows.append(Exchange(kv, qg, place, joined))
    for step in ("step0", "step1", "step2", "step3"):
        for flow in flows:
            getattr(flow, step)()
    outs = None
    parts = [local(arrays, layout, c * each, each) for c in range(chunks)]
    for c, flow in enumerate(flows):
        outs = final(arrays, parts[c], *flow.result(), layout, c * each, outs)
    return tuple(outs)


def solution(mesh):
    placed = P("seq", "head")
    return jax.shard_map(
        per_device,
        mesh=mesh,
        in_specs=(placed, placed, placed, placed, P()),
        out_specs=(placed, placed, placed, placed),
        check_vma=False,
    )
```

```python
import functools

import jax
import jax.numpy as jnp
from jax import lax
from jax.experimental import pallas as pl
from jax.experimental.pallas import tpu as pltpu
from jax.sharding import PartitionSpec as P

DH = 128
ROWS = 256
VMEM_LIMIT = 24 << 20
F32 = jnp.float32
LOW = jnp.bfloat16

NT = (((1,), (1,)), ((), ()))
TN = (((0,), (0,)), ((), ()))
NN = (((1,), (0,)), ((), ()))


def dot(a, b, dims):
    return lax.dot_general(a, b, dims, preferred_element_type=F32)


def split(a):
    high = a.astype(LOW)
    return high, (a - high.astype(F32)).astype(LOW)


def write_layout(lengths, offset, scale_ref, first_ref):
    count = scale_ref.shape[0]
    tiles = count // DH
    shape = (tiles, DH)
    row = lax.broadcasted_iota(jnp.int32, shape, 0) * DH + lax.broadcasted_iota(jnp.int32, shape, 1) + offset
    first = jnp.zeros(shape, jnp.int32)
    start = jnp.int32(0)
    for j in range(lengths.shape[0]):
        first = jnp.where(row >= start, start, first)
        start = start + lengths[j]
    scale = 1.0 / jnp.sqrt((row - first + 1).astype(F32) * DH)
    first = (first - offset).astype(F32)
    for t in range(tiles):
        rows = slice(t * DH, (t + 1) * DH)
        scale_ref[rows] = jnp.broadcast_to(scale[t : t + 1], (DH, DH)).T
        first_ref[rows] = jnp.broadcast_to(first[t : t + 1], (DH, DH)).T


def row_index(rows, base):
    return (lax.broadcasted_iota(jnp.int32, (rows, DH), 0) + base).astype(F32)


def key_values(k, v, first_ref, base, rows):
    start = first_ref[base + rows - 1 : base + rows]
    tail = jnp.where(row_index(rows, base) >= start, k, jnp.zeros((), LOW))
    return dot(tail, v, TN)


def query_grads(q, g, scale_ref, first_ref, base, rows):
    span = slice(base, base + rows)
    scaled = jnp.where(first_ref[span] < base, scale_ref[span] * g.astype(F32), 0.0)
    both = dot(q, jnp.concatenate(split(scaled), axis=1), TN)
    return both[:, :DH] + both[:, DH:]


def first_kernel(lengths, q_ref, k_ref, v_ref, g_ref, send_ref, scale_ref, first_ref):
    count = q_ref.shape[0]
    place = lax.axis_index("seq")

    @pl.when(pl.program_id(0) == 0)
    def _():
        write_layout(lengths, place * count, scale_ref, first_ref)

    @pl.when(place < 6)
    def _():
        send_ref[0] = key_values(k_ref[...], v_ref[...], first_ref, 0, count)

    @pl.when(place >= 6)
    def _():
        send_ref[0] = query_grads(q_ref[...], g_ref[...], scale_ref, first_ref, 0, count)


def goes_on(first_ref, base):
    return jnp.where(first_ref[base + ROWS - 1 : base + ROWS] < base, 1.0, 0.0)


def states_kernel(make_layout, lengths, q_ref, k_ref, v_ref, g_ref, *refs):
    count = q_ref.shape[0]
    if make_layout:
        kv_ref, qg_ref, inner_kv_ref, inner_qg_ref, scale_ref, first_ref = refs

        @pl.when(pl.program_id(0) == 0)
        def _():
            write_layout(lengths, lax.axis_index("seq") * count, scale_ref, first_ref)
    else:
        scale_ref, first_ref, kv_ref, qg_ref, inner_kv_ref, inner_qg_ref = refs
    bases = range(0, count, ROWS)
    total = None
    for c, base in enumerate(bases):
        span = slice(base, base + ROWS)
        part = key_values(k_ref[span], v_ref[span], first_ref, base, ROWS)
        total = part if total is None else total * goes_on(first_ref, base) + part
        if c < len(bases) - 1:
            inner_kv_ref[0, c] = total
    kv_ref[0] = total
    total = None
    for c, base in reversed(list(enumerate(bases))):
        span = slice(base, base + ROWS)
        part = query_grads(q_ref[span], g_ref[span], scale_ref, first_ref, base, ROWS)
        total = part if total is None else total * goes_on(first_ref, base) + part
        if c:
            inner_qg_ref[0, c - 1] = total
    qg_ref[0] = total


def local_kernel(q_ref, k_ref, v_ref, g_ref, scale_ref, first_ref, a_ref, dq_ref, dk_ref, dv_ref):
    count = q_ref.shape[0]
    many = ROWS // DH
    row = lax.broadcasted_iota(jnp.int32, (ROWS, ROWS), 0)
    col = lax.broadcasted_iota(jnp.int32, (ROWS, ROWS), 1)
    causal = col <= row
    col = col.astype(F32)
    for base in range(0, count, ROWS):
        rows = slice(base, base + ROWS)
        q, g, k, v = q_ref[rows], g_ref[rows], k_ref[rows], v_ref[rows]
        scale = scale_ref[rows]
        start = jnp.concatenate([first_ref[rows] - base] * many, axis=1)
        scale_w = jnp.concatenate([scale] * many, axis=1)
        mask = (col >= start) & causal
        scores = jnp.where(mask, dot(q, k, NT), 0.0).astype(LOW)
        grads = jnp.where(mask, dot(g, v, NT) * scale_w, 0.0).astype(LOW)
        scaled = (scale * g.astype(F32)).astype(LOW)
        a_ref[rows] = scale * dot(scores, v, NN)
        dq_ref[rows] = dot(grads, k, NN)
        dk_ref[rows] = dot(grads, q, TN)
        dv_ref[rows] = dot(scores, scaled, TN)


def final_kernel(
    q_ref, k_ref, v_ref, g_ref, a_ref, dq_ref, dk_ref, dv_ref, kv_ref, qg_ref, inner_kv_ref, inner_qg_ref,
    scale_ref, first_ref, *refs
):
    out_a, out_q, out_k, out_v = refs[-4:]
    count = q_ref.shape[0]
    bases = list(range(0, count, ROWS))

    def carried(rows, state, axis):
        both = jnp.concatenate(split(state), axis=axis)
        return dot(jnp.concatenate([rows, rows], axis=1), both, NT if axis else NN)

    kv_in = kv_ref[0]
    qg_in = qg_ref[0]
    keep = None
    for c, base in enumerate(bases):
        rows = slice(base, base + ROWS)
        if c == 0:
            state = kv_in
        else:
            went = goes_on(first_ref, bases[c - 1])
            keep = went if keep is None else keep * went
            state = kv_in * keep + inner_kv_ref[0, c - 1]
        scale = jnp.where(first_ref[rows] < base, scale_ref[rows], 0.0)
        out_a[rows] = (a_ref[rows] + scale * carried(q_ref[rows], state, 0)).astype(LOW)
        out_q[rows] = (dq_ref[rows] + scale * carried(g_ref[rows], state, 1)).astype(LOW)
    keep = None
    for c, base in reversed(list(enumerate(bases))):
        rows = slice(base, base + ROWS)
        if base == bases[-1]:
            state = qg_in
        else:
            went = goes_on(first_ref, bases[c + 1])
            keep = went if keep is None else keep * went
            state = qg_in * keep + inner_qg_ref[0, c]
        tail = row_index(ROWS, base) >= first_ref[base + ROWS - 1 : base + ROWS]
        out_k[rows] = (dk_ref[rows] + jnp.where(tail, carried(v_ref[rows], state, 1), 0.0)).astype(LOW)
        out_v[rows] = (dv_ref[rows] + jnp.where(tail, carried(k_ref[rows], state, 0), 0.0)).astype(LOW)


def head_block(count, base=None):
    return pl.BlockSpec((count, DH), lambda i, *_: (0, i if base is None else base() + i))


def whole(count):
    return pl.BlockSpec((count, DH), lambda i, *_: (0, 0))


def state_block(base=None):
    return pl.BlockSpec((1, DH, DH), lambda i, *_: (i if base is None else base() + i, 0, 0))


def inner_block(chunks, base=None):
    return pl.BlockSpec((1, chunks - 1, DH, DH), lambda i, *_: (i if base is None else base() + i, 0, 0, 0))


PARAMS = pltpu.CompilerParams(vmem_limit_bytes=VMEM_LIMIT)


def layout_shapes(count):
    return [jax.ShapeDtypeStruct((count, DH), F32)] * 2


def first_send(arrays, lengths, heads, base):
    count = arrays[0].shape[0]
    send, *layout = pl.pallas_call(
        first_kernel,
        out_shape=[jax.ShapeDtypeStruct((heads, DH, DH), F32)] + layout_shapes(count),
        grid_spec=pltpu.PrefetchScalarGridSpec(
            num_scalar_prefetch=1,
            grid=(heads,),
            in_specs=[head_block(count, base)] * 4,
            out_specs=[state_block()] + [whole(count)] * 2,
        ),
        compiler_params=PARAMS,
        name="first",
    )(lengths, *arrays)
    return send, tuple(layout)


def states(arrays, lengths, layout):
    count, width = arrays[0].shape
    heads = width // DH
    chunks = count // ROWS
    inner = jax.ShapeDtypeStruct((heads, chunks - 1, DH, DH), F32)
    out_shape = [jax.ShapeDtypeStruct((heads, DH, DH), F32)] * 2 + [inner] * 2
    out_specs = [state_block()] * 2 + [inner_block(chunks)] * 2
    in_specs = [head_block(count)] * 4
    if layout is None:
        out_shape += layout_shapes(count)
        out_specs += [whole(count)] * 2
    else:
        in_specs += [whole(count)] * 2
    return pl.pallas_call(
        functools.partial(states_kernel, layout is None),
        out_shape=out_shape,
        grid_spec=pltpu.PrefetchScalarGridSpec(
            num_scalar_prefetch=1, grid=(heads,), in_specs=in_specs, out_specs=out_specs
        ),
        compiler_params=PARAMS,
        name="states",
    )(lengths, *arrays, *(layout or ()))


def local(arrays, layout, heads, base):
    count = arrays[0].shape[0]
    shape = jax.ShapeDtypeStruct((count, heads * DH), F32)
    return pl.pallas_call(
        local_kernel,
        out_shape=[shape] * 4,
        grid=(heads,),
        in_specs=[head_block(count, base)] * 4 + [whole(count)] * 2,
        out_specs=[head_block(count)] * 4,
        compiler_params=PARAMS,
        name="local",
    )(*arrays, *layout)


def final(arrays, parts, kv, qg, inner, layout, base, outs):
    count, width = arrays[0].shape
    heads = kv.shape[0]
    chunks = count // ROWS
    shape = jax.ShapeDtypeStruct((count, width), LOW)
    extra = tuple(outs or ())
    return pl.pallas_call(
        final_kernel,
        out_shape=[shape] * 4,
        grid=(heads,),
        in_specs=[head_block(count, base)] * 4
        + [head_block(count)] * 4
        + [state_block()] * 2
        + [inner_block(chunks, base)] * 2
        + [whole(count)] * 2
        + [pl.BlockSpec(memory_space=pl.ANY)] * len(extra),
        out_specs=[head_block(count, base)] * 4,
        input_output_aliases={14 + i: i for i in range(len(extra))},
        compiler_params=PARAMS,
        name="final",
    )(*arrays, *parts, kv, qg, *inner, *layout, *extra)


PAIRS = [(d, d ^ 1) for d in range(8)]
UP_1 = [(0, 2), (2, 4), (3, 5)]
UP_2 = [(0, 2), (4, 6), (5, 7)]
DOWN_1 = [(2, 0), (6, 4), (7, 5)]
DOWN_2 = [(2, 0), (4, 2), (5, 3)]


def choose(place, default, *cases):
    value = default
    for devices, other in cases:
        hit = functools.reduce(jnp.logical_or, [place == d for d in devices])
        value = jnp.where(hit, other, value)
    return value


def permute(value, pairs):
    return lax.ppermute(value, "seq", pairs)


def on_eight(arrays, lengths):
    count, width = arrays[0].shape
    half = width // DH // 2
    d = lax.axis_index("seq")
    link = jnp.where(lengths[0] >= 2 * count, 1.0, 0.0)
    odd = d % 2 == 1

    def own():
        return lax.rem(lax.axis_index("seq"), 2) * half

    def other():
        return half - own()

    def given():
        place = lax.axis_index("seq")
        return jnp.where(place < 2, 0, half - lax.rem(place, 2) * half)

    send, layout = first_send(arrays, lengths, half, given)
    x0 = permute(send, PAIRS)
    kv, qg, *inner = states(arrays, lengths, layout)
    x0, kv, qg = lax.optimization_barrier((x0, kv, qg))
    k, q = (kv[:half], kv[half:]), (qg[:half], qg[half:])
    mine_k = jnp.where(odd, k[1], k[0])
    mine_q = jnp.where(odd, q[1], q[0])

    sum_k = mine_k + x0
    up = choose(d, sum_k, ((0,), x0 + link * k[0]))
    down = choose(d, mine_q + x0, ((2,), q[1]))
    up1 = permute(up, UP_1)
    down1 = permute(down, DOWN_1)
    send = choose(
        d, jnp.where(odd, q[0], q[1]), ((0, 1, 6), k[1]), ((2,), k[0]), ((3,), q[0]), ((7,), q[1])
    )
    x1 = permute(send, PAIRS)
    x0, *local_layout = lax.optimization_barrier((x0, *layout))
    own_parts = local(arrays, local_layout, half, own)
    up1, down1, x1, *own_parts = lax.optimization_barrier((up1, down1, x1, *own_parts))

    up = choose(d, up1 + sum_k, ((0,), x1 + link * k[1]))
    down = choose(d, down1 + mine_q + x1, ((2,), q[0]))
    up2 = permute(up, UP_2)
    down2 = permute(down, DOWN_2)
    send = choose(d, up1, ((0,), down1), ((1,), q[0]), ((4,), up1 + k[0]))
    x2 = permute(send, PAIRS)
    up1, *local_layout = lax.optimization_barrier((up1, *layout))
    other_parts = local(arrays, local_layout, half, other)
    up2, down2, x2, *other_parts = lax.optimization_barrier((up2, down2, x2, *other_parts))

    send = choose(
        d,
        down1,
        ((0, 2), down2),
        ((1,), q[1]),
        ((3,), down2 + q[1]),
        ((5,), down1 + q[1]),
        ((6,), up2 + k[0]),
        ((7,), up2),
    )
    x3 = permute(send, PAIRS)
    zero = jnp.zeros_like(x0)
    kv_own = choose(
        d, up1, ((0,), zero), ((1,), x1), ((3,), x0), ((5,), up1 + x0), ((6,), up2), ((7,), up2 + x1)
    )
    qg_own = choose(
        d,
        x0,
        ((0,), x2 + link * down2),
        ((1,), x2),
        ((2,), x1 + down2),
        ((3,), down2),
        ((4,), x1 + down1),
        ((5,), down1),
        ((7,), zero),
    )
    outs = final(arrays, own_parts, kv_own, qg_own, inner, layout, own, None)
    kv_other = choose(d, x3, ((0,), zero), ((1,), x0), ((2,), up2), ((3,), x1), ((4, 5), x2))
    qg_other = choose(d, x3, ((0,), x3 + link * down1), ((6,), x1), ((7,), zero))
    return tuple(final(arrays, other_parts, kv_other, qg_other, inner, layout, other, outs))


def on_any(arrays, lengths):
    count, width = arrays[0].shape
    heads = width // DH
    kv, qg, inner_kv, inner_qg, *layout = states(arrays, lengths, None)
    parts = local(arrays, layout, heads, None)
    starts_here = (layout[1][count - 1, 0] >= 0).astype(F32)
    kv_all, qg_all, start_all = lax.all_gather((kv, qg, starts_here), "seq")
    place = lax.axis_index("seq")
    devices = lax.axis_size("seq")
    order = jnp.arange(devices)
    last_start = jnp.max(jnp.where((order < place) & (start_all > 0.5), order, 0))
    next_start = jnp.min(jnp.where((order > place) & (start_all > 0.5), order, devices))

    def total(pick, values):
        return jnp.sum(jnp.where(pick[:, None, None, None], values, 0.0), axis=0)

    before = total((order < place) & (order >= last_start), kv_all)
    after = total((order > place) & (order <= next_start), qg_all)
    return tuple(final(arrays, parts, before, after, (inner_kv, inner_qg), layout, None, None))


def per_device(query_rows, key_rows, value_rows, grad_out, doc_lengths):
    arrays = (query_rows, key_rows, value_rows, grad_out)
    if lax.axis_size("seq") == 8:
        return on_eight(arrays, doc_lengths)
    return on_any(arrays, doc_lengths)


def solution(mesh):
    placed = P("seq", "head")
    return jax.shard_map(
        per_device,
        mesh=mesh,
        in_specs=(placed, placed, placed, placed, P()),
        out_specs=(placed, placed, placed, placed),
        check_vma=False,
    )
```

```python
import functools

import jax
import jax.numpy as jnp
from jax import lax
from jax.experimental import pallas as pl
from jax.experimental.pallas import tpu as pltpu
from jax.sharding import PartitionSpec as P

DH = 128
ROWS = 256
F32 = jnp.float32
LOW = jnp.bfloat16

NT = (((1,), (1,)), ((), ()))
TN = (((0,), (0,)), ((), ()))
NN = (((1,), (0,)), ((), ()))


def dot(a, b, dims):
    return lax.dot_general(a, b, dims, preferred_element_type=F32)


def split(a):
    high = a.astype(LOW)
    return high, (a - high.astype(F32)).astype(LOW)


def write_layout(lengths, offset, scale_ref, first_ref):
    count = scale_ref.shape[0]
    tiles = count // DH
    shape = (tiles, DH)
    row = lax.broadcasted_iota(jnp.int32, shape, 0) * DH + lax.broadcasted_iota(jnp.int32, shape, 1) + offset
    first = jnp.zeros(shape, jnp.int32)
    start = jnp.int32(0)
    for j in range(lengths.shape[0]):
        first = jnp.where(row >= start, start, first)
        start = start + lengths[j]
    scale = 1.0 / jnp.sqrt((row - first + 1).astype(F32) * DH)
    first = (first - offset).astype(F32)
    for t in range(tiles):
        rows = slice(t * DH, (t + 1) * DH)
        scale_ref[rows] = jnp.broadcast_to(scale[t : t + 1], (DH, DH)).T
        first_ref[rows] = jnp.broadcast_to(first[t : t + 1], (DH, DH)).T


def row_index(rows, base):
    return (lax.broadcasted_iota(jnp.int32, (rows, DH), 0) + base).astype(F32)


def key_values(k, v, start, base):
    tail = jnp.where(row_index(k.shape[0], base) >= start, k, jnp.zeros((), LOW))
    return dot(tail, v, TN)


def query_grads(q, g, scale, first, base):
    scaled = jnp.where(first < base, scale * g.astype(F32), 0.0)
    both = dot(q, jnp.concatenate(split(scaled), axis=1), TN)
    return both[:, :DH] + both[:, DH:]


def columns(h):
    return slice(h * DH, (h + 1) * DH)


def first_kernel(lengths, q_ref, k_ref, v_ref, g_ref, send_ref, scale_ref, first_ref):
    count = scale_ref.shape[0]
    place = lax.axis_index("seq")
    step = pl.program_id(0)
    base = pl.multiple_of(step * ROWS, ROWS)
    span = pl.ds(base, ROWS)

    @pl.when(step == 0)
    def _():
        write_layout(lengths, place * count, scale_ref, first_ref)
        send_ref[...] = jnp.zeros_like(send_ref)

    @pl.when(place < 6)
    def _():
        start = first_ref[count - 1 : count]
        for h in range(send_ref.shape[0]):
            cols = columns(h)
            send_ref[h] += key_values(k_ref[:, cols], v_ref[:, cols], start, base)

    @pl.when(place >= 6)
    def _():
        for h in range(send_ref.shape[0]):
            cols = columns(h)
            send_ref[h] += query_grads(q_ref[:, cols], g_ref[:, cols], scale_ref[span], first_ref[span], 0.0)


def states_kernel(make_layout, lengths, q_ref, k_ref, v_ref, g_ref, *refs):
    step = pl.program_id(0)
    last = pl.num_programs(0) - 1
    if make_layout:
        kv_ref, qg_ref, inner_kv_ref, inner_qg_ref, scale_ref, first_ref = refs
        count = scale_ref.shape[0]

        @pl.when(step == 0)
        def _():
            write_layout(lengths, lax.axis_index("seq") * count, scale_ref, first_ref)
    else:
        scale_ref, first_ref, kv_ref, qg_ref, inner_kv_ref, inner_qg_ref = refs

    @pl.when(step == 0)
    def _():
        kv_ref[...] = jnp.zeros_like(kv_ref)
        qg_ref[...] = jnp.zeros_like(qg_ref)

    down = pl.multiple_of(step * ROWS, ROWS)
    start = first_ref[pl.ds(down + ROWS - 1, 1)]
    keep = jnp.where(start < down.astype(F32), 1.0, 0.0)
    up = pl.multiple_of((last - step) * ROWS, ROWS)
    up_f = up.astype(F32)
    up_keep = jnp.where(first_ref[pl.ds(up + ROWS - 1, 1)] < up_f, 1.0, 0.0)
    scale, first = scale_ref[pl.ds(up, ROWS)], first_ref[pl.ds(up, ROWS)]
    for h in range(kv_ref.shape[0]):
        cols = columns(h)
        kv_ref[h] = kv_ref[h] * keep + key_values(k_ref[:, cols], v_ref[:, cols], start, down)
        qg_ref[h] = qg_ref[h] * up_keep + query_grads(q_ref[:, cols], g_ref[:, cols], scale, first, up_f)

    @pl.when(step < last)
    def _():
        inner_kv_ref[0] = kv_ref[...]
        inner_qg_ref[0] = qg_ref[...]


def local_kernel(q_ref, k_ref, v_ref, g_ref, scale_ref, first_ref, a_ref, dq_ref, dk_ref, dv_ref):
    many = ROWS // DH
    base = (pl.program_id(0) * ROWS).astype(F32)
    row = lax.broadcasted_iota(jnp.int32, (ROWS, ROWS), 0)
    col = lax.broadcasted_iota(jnp.int32, (ROWS, ROWS), 1)
    causal = col <= row
    col = col.astype(F32)
    for h in range(a_ref.shape[1] // DH):
        cols = columns(h)
        q, g, k, v = q_ref[:, cols], g_ref[:, cols], k_ref[:, cols], v_ref[:, cols]
        scale = scale_ref[...]
        start = jnp.concatenate([first_ref[...] - base] * many, axis=1)
        scale_w = jnp.concatenate([scale] * many, axis=1)
        mask = (col >= start) & causal
        scores = jnp.where(mask, dot(q, k, NT), 0.0).astype(LOW)
        grads = jnp.where(mask, dot(g, v, NT) * scale_w, 0.0).astype(LOW)
        scaled = (scale * g.astype(F32)).astype(LOW)
        a_ref[:, cols] = scale * dot(scores, v, NN)
        dq_ref[:, cols] = dot(grads, k, NN)
        dk_ref[:, cols] = dot(grads, q, TN)
        dv_ref[:, cols] = dot(scores, scaled, TN)


def final_kernel(
    q_ref, k_ref, v_ref, g_ref, a_ref, dq_ref, dk_ref, dv_ref, kv_ref, qg_ref, inner_kv_ref, inner_qg_ref,
    scale_ref, first_ref, *refs
):
    out_a, out_q, out_k, out_v = refs[-4:]
    count = scale_ref.shape[0]
    step = pl.program_id(0)
    last = pl.num_programs(0) - 1
    base = pl.multiple_of(step * ROWS, ROWS)
    base_f = base.astype(F32)
    span = pl.ds(base, ROWS)

    def carried(rows, state, axis):
        both = jnp.concatenate(split(state), axis=axis)
        return dot(jnp.concatenate([rows, rows], axis=1), both, NT if axis else NN)

    first = first_ref[span]
    scale = jnp.where(first < base_f, scale_ref[span], 0.0)
    tail = row_index(ROWS, base) >= first_ref[pl.ds(base + ROWS - 1, 1)]
    before = jnp.where(step > 0, 1.0, 0.0)
    after = jnp.where(step < last, 1.0, 0.0)
    whole_start = first_ref[pl.ds(jnp.maximum(base - 1, 0), 1)]
    kv_keep = jnp.where((whole_start < 0) | (step == 0), 1.0, 0.0)
    qg_keep = jnp.where(first_ref[count - 1 : count] < base_f + ROWS, 1.0, 0.0)
    for h in range(kv_ref.shape[0]):
        cols = columns(h)
        kv = kv_ref[h] * kv_keep + inner_kv_ref[0, h] * before
        qg = qg_ref[h] * qg_keep + inner_qg_ref[0, h] * after
        out_a[:, cols] = (a_ref[:, cols] + scale * carried(q_ref[:, cols], kv, 0)).astype(LOW)
        out_q[:, cols] = (dq_ref[:, cols] + scale * carried(g_ref[:, cols], kv, 1)).astype(LOW)
        out_k[:, cols] = (dk_ref[:, cols] + jnp.where(tail, carried(v_ref[:, cols], qg, 1), 0.0)).astype(LOW)
        out_v[:, cols] = (dv_ref[:, cols] + jnp.where(tail, carried(k_ref[:, cols], qg, 0), 0.0)).astype(LOW)


def at(part):
    return 0 if part is None else part()


def row_block(width, part=None, flip=None):
    return pl.BlockSpec((ROWS, width), lambda i, *_: (i if flip is None else flip - i, at(part)))


def layout_block():
    return pl.BlockSpec((ROWS, DH), lambda i, *_: (i, 0))


def whole(count):
    return pl.BlockSpec((count, DH), lambda i, *_: (0, 0))


def state_block(heads):
    return pl.BlockSpec((heads, DH, DH), lambda i, *_: (0, 0, 0))


def inner_block(heads, place, part=None):
    return pl.BlockSpec((1, heads, DH, DH), lambda i, *_: (place(i), at(part), 0, 0))


def layout_shapes(count):
    return [jax.ShapeDtypeStruct((count, DH), F32)] * 2


def first_send(arrays, lengths, heads, part):
    count = arrays[0].shape[0]
    send, *layout = pl.pallas_call(
        first_kernel,
        out_shape=[jax.ShapeDtypeStruct((heads, DH, DH), F32)] + layout_shapes(count),
        grid_spec=pltpu.PrefetchScalarGridSpec(
            num_scalar_prefetch=1,
            grid=(count // ROWS,),
            in_specs=[row_block(heads * DH, part)] * 4,
            out_specs=[state_block(heads)] + [whole(count)] * 2,
        ),
        name="first",
    )(lengths, *arrays)
    return send, tuple(layout)


def states(arrays, lengths, layout):
    count, width = arrays[0].shape
    heads = width // DH
    chunks = count // ROWS
    inner = jax.ShapeDtypeStruct((chunks - 1, heads, DH, DH), F32)
    out_shape = [jax.ShapeDtypeStruct((heads, DH, DH), F32)] * 2 + [inner] * 2
    out_specs = [state_block(heads)] * 2 + [
        inner_block(heads, lambda i: jnp.minimum(i, chunks - 2)),
        inner_block(heads, lambda i: jnp.maximum(chunks - 2 - i, 0)),
    ]
    back = row_block(width, None, chunks - 1)
    in_specs = [back, row_block(width), row_block(width), back]
    if layout is None:
        out_shape += layout_shapes(count)
        out_specs += [whole(count)] * 2
    else:
        in_specs += [whole(count)] * 2
    return pl.pallas_call(
        functools.partial(states_kernel, layout is None),
        out_shape=out_shape,
        grid_spec=pltpu.PrefetchScalarGridSpec(
            num_scalar_prefetch=1, grid=(chunks,), in_specs=in_specs, out_specs=out_specs
        ),
        name="states",
    )(lengths, *arrays, *(layout or ()))


def local(arrays, layout, heads, part):
    count = arrays[0].shape[0]
    shape = jax.ShapeDtypeStruct((count, heads * DH), F32)
    return pl.pallas_call(
        local_kernel,
        out_shape=[shape] * 4,
        grid=(count // ROWS,),
        in_specs=[row_block(heads * DH, part)] * 4 + [layout_block()] * 2,
        out_specs=[row_block(heads * DH)] * 4,
        name="local",
    )(*arrays, *layout)


def final(arrays, parts, kv, qg, inner, layout, part, outs):
    count, width = arrays[0].shape
    heads = kv.shape[0]
    chunks = count // ROWS
    shape = jax.ShapeDtypeStruct((count, width), LOW)
    extra = tuple(outs or ())
    return pl.pallas_call(
        final_kernel,
        out_shape=[shape] * 4,
        grid=(chunks,),
        in_specs=[row_block(heads * DH, part)] * 4
        + [row_block(heads * DH)] * 4
        + [state_block(heads)] * 2
        + [
            inner_block(heads, lambda i: jnp.maximum(i - 1, 0), part),
            inner_block(heads, lambda i: jnp.minimum(i, chunks - 2), part),
        ]
        + [whole(count)] * 2
        + [pl.BlockSpec(memory_space=pl.ANY)] * len(extra),
        out_specs=[row_block(heads * DH, part)] * 4,
        input_output_aliases={14 + i: i for i in range(len(extra))},
        name="final",
    )(*arrays, *parts, kv, qg, *inner, *layout, *extra)


PAIRS = [(d, d ^ 1) for d in range(8)]
UP_1 = [(0, 2), (2, 4), (3, 5)]
UP_2 = [(0, 2), (4, 6), (5, 7)]
DOWN_1 = [(2, 0), (6, 4), (7, 5)]
DOWN_2 = [(2, 0), (4, 2), (5, 3)]


def choose(place, default, *cases):
    value = default
    for devices, other in cases:
        hit = functools.reduce(jnp.logical_or, [place == d for d in devices])
        value = jnp.where(hit, other, value)
    return value


def permute(value, pairs):
    return lax.ppermute(value, "seq", pairs)


def on_eight(arrays, lengths):
    count, width = arrays[0].shape
    half = width // DH // 2
    d = lax.axis_index("seq")
    link = jnp.where(lengths[0] >= 2 * count, 1.0, 0.0)
    odd = d % 2 == 1

    def own():
        return lax.rem(lax.axis_index("seq"), 2)

    def other():
        return 1 - own()

    def given():
        return jnp.where(lax.axis_index("seq") < 2, 0, other())

    send, layout = first_send(arrays, lengths, half, given)
    x0 = permute(send, PAIRS)
    kv, qg, *inner = states(arrays, lengths, layout)
    x0, kv, qg = lax.optimization_barrier((x0, kv, qg))
    k, q = (kv[:half], kv[half:]), (qg[:half], qg[half:])
    mine_k = jnp.where(odd, k[1], k[0])
    mine_q = jnp.where(odd, q[1], q[0])

    sum_k = mine_k + x0
    up = choose(d, sum_k, ((0,), x0 + link * k[0]))
    down = choose(d, mine_q + x0, ((2,), q[1]))
    up1 = permute(up, UP_1)
    down1 = permute(down, DOWN_1)
    send = choose(
        d, jnp.where(odd, q[0], q[1]), ((0, 1, 6), k[1]), ((2,), k[0]), ((3,), q[0]), ((7,), q[1])
    )
    x1 = permute(send, PAIRS)
    x0, *local_layout = lax.optimization_barrier((x0, *layout))
    own_parts = local(arrays, local_layout, half, own)
    up1, down1, x1, *own_parts = lax.optimization_barrier((up1, down1, x1, *own_parts))

    up = choose(d, up1 + sum_k, ((0,), x1 + link * k[1]))
    down = choose(d, down1 + mine_q + x1, ((2,), q[0]))
    up2 = permute(up, UP_2)
    down2 = permute(down, DOWN_2)
    send = choose(d, up1, ((0,), down1), ((1,), q[0]), ((4,), up1 + k[0]))
    x2 = permute(send, PAIRS)
    up1, *local_layout = lax.optimization_barrier((up1, *layout))
    other_parts = local(arrays, local_layout, half, other)
    up2, down2, x2, *other_parts = lax.optimization_barrier((up2, down2, x2, *other_parts))

    send = choose(
        d,
        down1,
        ((0, 2), down2),
        ((1,), q[1]),
        ((3,), down2 + q[1]),
        ((5,), down1 + q[1]),
        ((6,), up2 + k[0]),
        ((7,), up2),
    )
    x3 = permute(send, PAIRS)
    zero = jnp.zeros_like(x0)
    kv_own = choose(
        d, up1, ((0,), zero), ((1,), x1), ((3,), x0), ((5,), up1 + x0), ((6,), up2), ((7,), up2 + x1)
    )
    qg_own = choose(
        d,
        x0,
        ((0,), x2 + link * down2),
        ((1,), x2),
        ((2,), x1 + down2),
        ((3,), down2),
        ((4,), x1 + down1),
        ((5,), down1),
        ((7,), zero),
    )
    outs = final(arrays, own_parts, kv_own, qg_own, inner, layout, own, None)
    x3, *outs = lax.optimization_barrier((x3, *outs))
    kv_other = choose(d, x3, ((0,), zero), ((1,), x0), ((2,), up2), ((3,), x1), ((4, 5), x2))
    qg_other = choose(d, x3, ((0,), x3 + link * down1), ((6,), x1), ((7,), zero))
    return tuple(final(arrays, other_parts, kv_other, qg_other, inner, layout, other, outs))


def on_any(arrays, lengths):
    count, width = arrays[0].shape
    heads = width // DH
    kv, qg, inner_kv, inner_qg, *layout = states(arrays, lengths, None)
    parts = local(arrays, layout, heads, None)
    starts_here = (layout[1][count - 1, 0] >= 0).astype(F32)
    kv_all, qg_all, start_all = lax.all_gather((kv, qg, starts_here), "seq")
    place = lax.axis_index("seq")
    devices = lax.axis_size("seq")
    order = jnp.arange(devices)
    last_start = jnp.max(jnp.where((order < place) & (start_all > 0.5), order, 0))
    next_start = jnp.min(jnp.where((order > place) & (start_all > 0.5), order, devices))

    def total(pick, values):
        return jnp.sum(jnp.where(pick[:, None, None, None], values, 0.0), axis=0)

    before = total((order < place) & (order >= last_start), kv_all)
    after = total((order > place) & (order <= next_start), qg_all)
    return tuple(final(arrays, parts, before, after, (inner_kv, inner_qg), layout, None, None))


def per_device(query_rows, key_rows, value_rows, grad_out, doc_lengths):
    arrays = (query_rows, key_rows, value_rows, grad_out)
    if lax.axis_size("seq") == 8:
        return on_eight(arrays, doc_lengths)
    return on_any(arrays, doc_lengths)


def solution(mesh):
    placed = P("seq", "head")
    return jax.shard_map(
        per_device,
        mesh=mesh,
        in_specs=(placed, placed, placed, placed, P()),
        out_specs=(placed, placed, placed, placed),
        check_vma=False,
    )
```

```python
import functools

import jax
import jax.numpy as jnp
from jax import lax
from jax.experimental import pallas as pl
from jax.experimental.pallas import tpu as pltpu
from jax.sharding import PartitionSpec as P

DH = 128
ROWS = 256
VMEM_LIMIT = 16 << 20
F32 = jnp.float32
LOW = jnp.bfloat16

NT = (((1,), (1,)), ((), ()))
TN = (((0,), (0,)), ((), ()))
NN = (((1,), (0,)), ((), ()))


def dot(a, b, dims):
    return lax.dot_general(a, b, dims, preferred_element_type=F32)


def split(a):
    high = a.astype(LOW)
    return high, (a - high.astype(F32)).astype(LOW)


def write_layout(lengths, offset, scale_ref, first_ref):
    count = scale_ref.shape[0]
    tiles = count // DH
    shape = (tiles, DH)
    row = lax.broadcasted_iota(jnp.int32, shape, 0) * DH + lax.broadcasted_iota(jnp.int32, shape, 1) + offset
    first = jnp.zeros(shape, jnp.int32)
    start = jnp.int32(0)
    for j in range(lengths.shape[0]):
        first = jnp.where(row >= start, start, first)
        start = start + lengths[j]
    scale = 1.0 / jnp.sqrt((row - first + 1).astype(F32) * DH)
    first = (first - offset).astype(F32)
    for t in range(tiles):
        rows = slice(t * DH, (t + 1) * DH)
        scale_ref[rows] = jnp.broadcast_to(scale[t : t + 1], (DH, DH)).T
        first_ref[rows] = jnp.broadcast_to(first[t : t + 1], (DH, DH)).T


def row_index(rows, base):
    return (lax.broadcasted_iota(jnp.int32, (rows, DH), 0) + base).astype(F32)


def key_values(k, v, start, base):
    tail = jnp.where(row_index(k.shape[0], base) >= start, k, jnp.zeros((), LOW))
    return dot(tail, v, TN)


def query_grads(q, g, scale, first, base):
    scaled = jnp.where(first < base, scale * g.astype(F32), 0.0)
    both = dot(q, jnp.concatenate(split(scaled), axis=1), TN)
    return both[:, :DH] + both[:, DH:]


def columns(h):
    return slice(h * DH, (h + 1) * DH)


def first_kernel(
    lengths_hbm, q_hbm, k_hbm, v_hbm, g_hbm, send_ref, scale_ref, first_ref, link_ref, lengths, left, right, sems, sem
):
    lengths_copy = pltpu.make_async_copy(lengths_hbm, lengths, sem)
    lengths_copy.start()
    count = scale_ref.shape[0]
    place = lax.axis_index("seq")
    width = left.shape[1]
    part = jnp.where(place < 2, 0, 1 - lax.rem(place, 2)) * width
    pieces = width // (2 * DH)

    def copies(sources):
        made = []
        for piece in range(pieces):
            for n, (source, target) in enumerate(zip(sources, (left, right))):
                column = pl.multiple_of(part + piece * 2 * DH, DH)
                made.append(
                    pltpu.make_async_copy(
                        source.at[:, pl.ds(column, 2 * DH)],
                        target.at[:, piece * 2 * DH : (piece + 1) * 2 * DH],
                        sems.at[n, piece],
                    )
                )
        return made

    def run(sources, total):
        made = copies(sources)
        for piece in range(pieces):
            made[2 * piece].wait()
            made[2 * piece + 1].wait()
            for h in (2 * piece, 2 * piece + 1):
                send_ref[h] = total(left[:, columns(h)], right[:, columns(h)])

    keys = place < 6

    @pl.when(keys)
    def _():
        for copy in copies((k_hbm, v_hbm)):
            copy.start()

    @pl.when(jnp.logical_not(keys))
    def _():
        for copy in copies((q_hbm, g_hbm)):
            copy.start()

    lengths_copy.wait()
    write_layout(lengths, place * count, scale_ref, first_ref)
    link_ref[...] = jnp.full(link_ref.shape, jnp.where(lengths[0] >= 2 * count, 1.0, 0.0), F32)

    @pl.when(keys)
    def _():
        start = first_ref[count - 1 : count]
        run((k_hbm, v_hbm), lambda k, v: key_values(k, v, start, 0))

    @pl.when(jnp.logical_not(keys))
    def _():
        run((q_hbm, g_hbm), lambda q, g: query_grads(q, g, scale_ref[...], first_ref[...], 0.0))


def states_kernel(q_hbm, k_hbm, v_hbm, g_hbm, scale_ref, first_ref, *refs):
    kv_ref, qg_ref, inner_kv_ref, inner_qg_ref, q_ref, k_ref, v_ref, g_ref, sems = refs
    count = q_ref.shape[0]
    chunks = count // ROWS
    steps = []
    for step in range(chunks):
        down, up = step * ROWS, (chunks - 1 - step) * ROWS
        made = []
        for n, (source, target, base) in enumerate(
            ((k_hbm, k_ref, down), (v_hbm, v_ref, down), (q_hbm, q_ref, up), (g_hbm, g_ref, up))
        ):
            rows = slice(base, base + ROWS)
            made.append(pltpu.make_async_copy(source.at[rows], target.at[rows], sems.at[n, step]))
        steps.append(made)
    for made in steps:
        for copy in made:
            copy.start()
    for step, made in enumerate(steps):
        for copy in made:
            copy.wait()
        down, up = step * ROWS, (chunks - 1 - step) * ROWS
        rows, back = slice(down, down + ROWS), slice(up, up + ROWS)
        start = first_ref[down + ROWS - 1 : down + ROWS]
        keep = jnp.where(start < down, 1.0, 0.0)
        up_keep = jnp.where(first_ref[up + ROWS - 1 : up + ROWS] < up, 1.0, 0.0)
        for h in range(kv_ref.shape[0]):
            cols = columns(h)
            kv = key_values(k_ref[rows, cols], v_ref[rows, cols], start, down)
            qg = query_grads(q_ref[back, cols], g_ref[back, cols], scale_ref[back], first_ref[back], up)
            if step:
                kv = inner_kv_ref[step - 1, h] * keep + kv
                qg = inner_qg_ref[chunks - 1 - step, h] * up_keep + qg
            if step < chunks - 1:
                inner_kv_ref[step, h] = kv
                inner_qg_ref[chunks - 2 - step, h] = qg
            else:
                kv_ref[h] = kv
                qg_ref[h] = qg


def part_columns(part, width, h):
    return pl.ds(pl.multiple_of(part * width + h * DH, DH), DH)


def local_kernel(pick, q_ref, k_ref, v_ref, g_ref, scale_ref, first_ref, tie_ref, a_ref, dq_ref, dk_ref, dv_ref):
    del tie_ref
    many = ROWS // DH
    count, width = a_ref.shape
    part = pick()
    row = lax.broadcasted_iota(jnp.int32, (ROWS, ROWS), 0)
    col = lax.broadcasted_iota(jnp.int32, (ROWS, ROWS), 1)
    causal = col <= row
    col = col.astype(F32)

    def chunk(c, _):
        base = pl.multiple_of(c * ROWS, ROWS)
        rows = pl.ds(base, ROWS)
        base = base.astype(F32)
        for h in range(width // DH):
            cols = part_columns(part, width, h)
            to = columns(h)
            q, g, k, v = q_ref[rows, cols], g_ref[rows, cols], k_ref[rows, cols], v_ref[rows, cols]
            scale = scale_ref[rows]
            start = jnp.concatenate([first_ref[rows] - base] * many, axis=1)
            scale_w = jnp.concatenate([scale] * many, axis=1)
            mask = (col >= start) & causal
            scores = jnp.where(mask, dot(q, k, NT), 0.0).astype(LOW)
            grads = jnp.where(mask, dot(g, v, NT) * scale_w, 0.0).astype(LOW)
            scaled = (scale * g.astype(F32)).astype(LOW)
            a_ref[rows, to] = scale * dot(scores, v, NN)
            dq_ref[rows, to] = dot(grads, k, NN)
            dk_ref[rows, to] = dot(grads, q, TN)
            dv_ref[rows, to] = dot(scores, scaled, TN)
        return 0

    lax.fori_loop(0, count // ROWS, chunk, 0)


def final_kernel(
    gather, pick, inputs, aliased, q_ref, k_ref, v_ref, g_ref, a_ref, dq_ref, dk_ref, dv_ref,
    inner_kv_ref, inner_qg_ref, scale_ref, first_ref, *refs
):
    taken = refs[:inputs]
    outs = refs[inputs + aliased : inputs + aliased + 4]
    *kept, kv_ref, qg_ref, sems = refs[inputs + aliased + 4 :]
    out_a, out_q, out_k, out_v = kept
    gather(kv_ref, qg_ref, *taken)
    count, width = out_a.shape
    chunks = count // ROWS
    heads = kv_ref.shape[0]
    part = pick()

    def carried(rows, state, axis):
        both = jnp.concatenate(split(state), axis=axis)
        return dot(jnp.concatenate([rows, rows], axis=1), both, NT if axis else NN)

    copies = []
    for c in range(chunks):
        base = c * ROWS
        rows = slice(base, base + ROWS)
        first = first_ref[rows]
        scale = jnp.where(first < base, scale_ref[rows], 0.0)
        tail = row_index(ROWS, base) >= first_ref[base + ROWS - 1 : base + ROWS]
        for h in range(heads):
            cols = part_columns(part, width, h)
            to = columns(h)
            kv, qg = kv_ref[h], qg_ref[h]
            if c:
                kept_on = jnp.where(first_ref[base - 1 : base] < 0, 1.0, 0.0)
                kv = kv * kept_on + inner_kv_ref[c - 1, part * heads + h]
            if c < chunks - 1:
                kept_on = jnp.where(first_ref[count - 1 : count] < base + ROWS, 1.0, 0.0)
                qg = qg * kept_on + inner_qg_ref[c, part * heads + h]
            out_a[rows, to] = (a_ref[rows, to] + scale * carried(q_ref[rows, cols], kv, 0)).astype(LOW)
            out_q[rows, to] = (dq_ref[rows, to] + scale * carried(g_ref[rows, cols], kv, 1)).astype(LOW)
            out_k[rows, to] = (dk_ref[rows, to] + jnp.where(tail, carried(v_ref[rows, cols], qg, 1), 0.0)).astype(LOW)
            out_v[rows, to] = (dv_ref[rows, to] + jnp.where(tail, carried(k_ref[rows, cols], qg, 0), 0.0)).astype(LOW)
        for n, (kept_ref, out) in enumerate(zip(kept, outs)):
            target = out.at[rows, pl.ds(pl.multiple_of(part * width, DH), width)]
            copies.append(pltpu.make_async_copy(kept_ref.at[rows], target, sems.at[n, c]))
            copies[-1].start()
    for copy in copies:
        copy.wait()


IN_VMEM = pl.BlockSpec(memory_space=pltpu.VMEM)
IN_HBM = pl.BlockSpec(memory_space=pltpu.HBM)
PARAMS = pltpu.CompilerParams(vmem_limit_bytes=VMEM_LIMIT)


def call(kernel, name, out_shape, in_specs, out_specs, scratch=(), aliases=None):
    return pl.pallas_call(
        kernel,
        out_shape=out_shape,
        in_specs=in_specs,
        out_specs=out_specs,
        scratch_shapes=scratch,
        input_output_aliases=aliases or {},
        compiler_params=PARAMS,
        name=name,
    )


def sums_shape(heads, *lead):
    return jax.ShapeDtypeStruct((*lead, heads, DH, DH), F32)


def first_send(arrays, lengths, heads):
    count = arrays[0].shape[0]
    width = heads * DH
    row = jax.ShapeDtypeStruct((count, DH), F32)
    return call(
        first_kernel,
        "first",
        [sums_shape(heads), row, row, jax.ShapeDtypeStruct((DH, DH), F32)],
        [IN_HBM] * 5,
        [IN_VMEM] * 4,
        [pltpu.SMEM(lengths.shape, jnp.int32)]
        + [pltpu.VMEM((count, width), LOW)] * 2
        + [pltpu.SemaphoreType.DMA((2, heads // 2)), pltpu.SemaphoreType.DMA(())],
    )(lengths, *arrays)


def states(arrays, layout):
    count, width = arrays[0].shape
    heads = width // DH
    chunks = count // ROWS
    outs = call(
        states_kernel,
        "states",
        [sums_shape(heads)] * 2
        + [sums_shape(heads, chunks - 1)] * 2
        + [jax.ShapeDtypeStruct((count, width), LOW)] * 4,
        [IN_HBM] * 4 + [IN_VMEM] * 2,
        [IN_VMEM] * 8,
        [pltpu.SemaphoreType.DMA((4, chunks))],
    )(*arrays, *layout)
    return outs[:4], outs[4:]


def local(arrays, layout, heads, pick, tie):
    count = arrays[0].shape[0]
    shape = jax.ShapeDtypeStruct((count, heads * DH), F32)
    return call(
        functools.partial(local_kernel, pick),
        "local",
        [shape] * 4,
        [IN_VMEM] * 6 + [pl.BlockSpec(memory_space=pl.ANY)],
        [IN_VMEM] * 4,
    )(*arrays, *layout, tie)


def final(arrays, parts, inner, layout, gather, pick, taken, outs):
    count, width = arrays[0].shape
    chunks, part_width = count // ROWS, parts[0].shape[1]
    heads = part_width // DH
    extra = tuple(outs or ())
    at = 12 + len(taken)
    return call(
        functools.partial(final_kernel, gather, pick, len(taken), len(extra)),
        "final",
        [jax.ShapeDtypeStruct((count, width), LOW)] * 4,
        [IN_VMEM] * at + [IN_HBM] * len(extra),
        [IN_HBM] * 4,
        [pltpu.VMEM((count, part_width), LOW)] * 4
        + [pltpu.VMEM((heads, DH, DH), F32)] * 2
        + [pltpu.SemaphoreType.DMA((4, chunks))],
        {at + i: i for i in range(len(extra))},
    )(*arrays, *parts, *inner, *layout, *taken, *extra)


PAIRS = [(d, d ^ 1) for d in range(8)]
PAIRS_2 = [(0, 1), (1, 0), (4, 5), (5, 4)]
UP_1 = [(0, 2), (2, 4), (3, 5)]
UP_2 = [(0, 2), (4, 6), (5, 7)]
DOWN_1 = [(2, 0), (6, 4), (7, 5)]
DOWN_2 = [(2, 0), (4, 2), (5, 3)]


def put(ref, *cases):
    place = lax.axis_index("seq")
    for devices, value in cases:
        hit = functools.reduce(jnp.logical_or, [place == d for d in devices])

        @pl.when(hit)
        def _():
            ref[...] = value()


def permute(value, pairs):
    return lax.ppermute(value, "seq", pairs)


def select(kernel, name, outs, *taken):
    heads = taken[0].shape[0]
    return call(kernel, name, [sums_shape(heads)] * outs, [IN_VMEM] * len(taken), [IN_VMEM] * outs)(*taken)


def own():
    return lax.rem(lax.axis_index("seq"), 2)


def other():
    return 1 - own()


def on_eight(arrays, lengths):
    count, width = arrays[0].shape
    heads = width // DH
    half = heads // 2
    low, high = slice(0, half), slice(half, heads)

    def select_1(x0, link, kv, qg, up, down, send):
        put(
            up,
            ((0,), lambda: x0[...] + link[...] * kv[low]),
            ((2, 4), lambda: x0[...] + kv[low]),
            ((3, 5), lambda: x0[...] + kv[high]),
        )
        put(
            down,
            ((2,), lambda: qg[high]),
            ((6,), lambda: x0[...] + qg[low]),
            ((7,), lambda: x0[...] + qg[high]),
        )
        put(
            send,
            ((0, 1, 6), lambda: kv[high]),
            ((2,), lambda: kv[low]),
            ((3, 5), lambda: qg[low]),
            ((4, 7), lambda: qg[high]),
        )

    def select_2(x0, x1, link, up1, down1, kv, qg, up, down, send):
        put(
            up,
            ((0,), lambda: x1[...] + link[...] * kv[high]),
            ((4,), lambda: up1[...] + (x0[...] + kv[low])),
            ((5,), lambda: up1[...] + (x0[...] + kv[high])),
        )
        put(
            down,
            ((2,), lambda: qg[low]),
            ((4,), lambda: down1[...] + (x1[...] + qg[low])),
            ((5,), lambda: down1[...] + (x1[...] + qg[high])),
        )
        put(
            send,
            ((0,), lambda: down1[...]),
            ((1,), lambda: qg[low]),
            ((4,), lambda: up1[...] + kv[low]),
            ((5,), lambda: up1[...]),
        )

    def select_3(down1, up2, down2, kv, qg, send):
        put(
            send,
            ((0, 2), lambda: down2[...]),
            ((1,), lambda: qg[high]),
            ((3,), lambda: down2[...] + qg[high]),
            ((4,), lambda: down1[...]),
            ((5,), lambda: down1[...] + qg[high]),
            ((6,), lambda: up2[...] + kv[low]),
            ((7,), lambda: up2[...]),
        )

    def gather_own(kv, qg, link, x0, x1, x2, up1, down1, up2, down2):
        put(
            kv,
            ((0,), lambda: jnp.zeros_like(kv)),
            ((1,), lambda: x1[...]),
            ((2, 4), lambda: up1[...]),
            ((3,), lambda: x0[...]),
            ((5,), lambda: up1[...] + x0[...]),
            ((6,), lambda: up2[...]),
            ((7,), lambda: up2[...] + x1[...]),
        )
        put(
            qg,
            ((0,), lambda: x2[...] + link[...] * down2[...]),
            ((1,), lambda: x2[...]),
            ((2,), lambda: x1[...] + down2[...]),
            ((3,), lambda: down2[...]),
            ((4,), lambda: x1[...] + down1[...]),
            ((5,), lambda: down1[...]),
            ((6,), lambda: x0[...]),
            ((7,), lambda: jnp.zeros_like(qg)),
        )

    def gather_other(kv, qg, link, x0, x1, x2, x3, down1, up2):
        put(
            kv,
            ((0,), lambda: jnp.zeros_like(kv)),
            ((1,), lambda: x0[...]),
            ((2,), lambda: up2[...]),
            ((3,), lambda: x1[...]),
            ((4, 5), lambda: x2[...]),
            ((6, 7), lambda: x3[...]),
        )
        put(
            qg,
            ((0,), lambda: x3[...] + link[...] * down1[...]),
            ((1, 2, 3, 4, 5), lambda: x3[...]),
            ((6,), lambda: x1[...]),
            ((7,), lambda: jnp.zeros_like(qg)),
        )

    send, *layout, link = first_send(arrays, lengths, half)
    x0 = permute(send, PAIRS)
    (kv, qg, *inner), arrays = states(arrays, layout)
    x0, kv, qg = lax.optimization_barrier((x0, kv, qg))
    up, down, send = select(select_1, "select1", 3, x0, link, kv, qg)
    x1, up1, down1 = permute(send, PAIRS), permute(up, UP_1), permute(down, DOWN_1)
    own_parts = local(arrays, layout, half, own, send)
    x1, up1, down1, *own_parts = lax.optimization_barrier((x1, up1, down1, *own_parts))
    up, down, send = select(select_2, "select2", 3, x0, x1, link, up1, down1, kv, qg)
    x2, up2, down2 = permute(send, PAIRS_2), permute(up, UP_2), permute(down, DOWN_2)
    other_parts = local(arrays, layout, half, other, send)
    x2, up2, down2, *other_parts = lax.optimization_barrier((x2, up2, down2, *other_parts))
    (send,) = select(select_3, "select3", 1, down1, up2, down2, kv, qg)
    x3 = permute(send, PAIRS)
    outs = final(
        arrays, own_parts, inner, layout, gather_own, own, (link, x0, x1, x2, up1, down1, up2, down2), None
    )
    x3, *outs = lax.optimization_barrier((x3, *outs))
    return tuple(
        final(
            arrays, other_parts, inner, layout, gather_other, other, (link, x0, x1, x2, x3, down1, up2), outs
        )
    )


def on_any(arrays, lengths):
    count, width = arrays[0].shape
    heads = width // DH
    _, *layout, _ = first_send(arrays, lengths, heads // 2)
    (kv, qg, *inner), arrays = states(arrays, layout)
    parts = local(arrays, layout, heads, lambda: jnp.int32(0), kv)
    starts_here = (layout[1][count - 1, 0] >= 0).astype(F32)
    kv_all, qg_all, start_all = lax.all_gather((kv, qg, starts_here), "seq")
    place = lax.axis_index("seq")
    devices = lax.axis_size("seq")
    order = jnp.arange(devices)
    last_start = jnp.max(jnp.where((order < place) & (start_all > 0.5), order, 0))
    next_start = jnp.min(jnp.where((order > place) & (start_all > 0.5), order, devices))

    def total(pick, values):
        return jnp.sum(jnp.where(pick[:, None, None, None], values, 0.0), axis=0)

    def gather(kv_ref, qg_ref, before, after):
        kv_ref[...] = before[...]
        qg_ref[...] = after[...]

    before = total((order < place) & (order >= last_start), kv_all)
    after = total((order > place) & (order <= next_start), qg_all)
    return tuple(final(arrays, parts, inner, layout, gather, lambda: jnp.int32(0), (before, after), None))


def per_device(query_rows, key_rows, value_rows, grad_out, doc_lengths):
    *arrays, doc_lengths = (
        pltpu.with_memory_space_constraint(a, pltpu.HBM)
        for a in (query_rows, key_rows, value_rows, grad_out, doc_lengths)
    )
    if lax.axis_size("seq") == 8:
        return on_eight(arrays, doc_lengths)
    return on_any(arrays, doc_lengths)


def solution(mesh):
    placed = P("seq", "head")
    return jax.shard_map(
        per_device,
        mesh=mesh,
        in_specs=(placed, placed, placed, placed, P()),
        out_specs=(placed, placed, placed, placed),
        check_vma=False,
    )
```

```python
import functools

import jax
import jax.numpy as jnp
from jax import lax
from jax.experimental import pallas as pl
from jax.experimental.pallas import tpu as pltpu
from jax.sharding import PartitionSpec as P

DH = 128
ROWS = 256
VMEM_LIMIT = 16 << 20
F32 = jnp.float32
LOW = jnp.bfloat16

NT = (((1,), (1,)), ((), ()))
TN = (((0,), (0,)), ((), ()))
NN = (((1,), (0,)), ((), ()))


def dot(a, b, dims):
    return lax.dot_general(a, b, dims, preferred_element_type=F32)


def split(a):
    high = a.astype(LOW)
    return high, (a - high.astype(F32)).astype(LOW)


def write_layout(lengths, offset, scale_ref, first_ref):
    count = scale_ref.shape[0]
    tiles = count // DH
    shape = (tiles, DH)
    row = lax.broadcasted_iota(jnp.int32, shape, 0) * DH + lax.broadcasted_iota(jnp.int32, shape, 1) + offset
    first = jnp.zeros(shape, jnp.int32)
    start = jnp.int32(0)
    for j in range(lengths.shape[0]):
        first = jnp.where(row >= start, start, first)
        start = start + lengths[j]
    scale = 1.0 / jnp.sqrt((row - first + 1).astype(F32) * DH)
    first = (first - offset).astype(F32)
    for t in range(tiles):
        rows = slice(t * DH, (t + 1) * DH)
        scale_ref[rows] = jnp.broadcast_to(scale[t : t + 1], (DH, DH)).T
        first_ref[rows] = jnp.broadcast_to(first[t : t + 1], (DH, DH)).T


def row_index(rows, base):
    return (lax.broadcasted_iota(jnp.int32, (rows, DH), 0) + base).astype(F32)


def key_values(k, v, start, base):
    tail = jnp.where(row_index(k.shape[0], base) >= start, k, jnp.zeros((), LOW))
    return dot(tail, v, TN)


def query_grads(q, g, scale, first, base):
    scaled = jnp.where(first < base, scale * g.astype(F32), 0.0)
    both = dot(q, jnp.concatenate(split(scaled), axis=1), TN)
    return both[:, :DH] + both[:, DH:]


def columns(h):
    return slice(h * DH, (h + 1) * DH)


def first_kernel(
    lengths_hbm, q_hbm, k_hbm, v_hbm, g_hbm, send_ref, scale_ref, first_ref, link_ref, lengths, left, right, sems, sem
):
    lengths_copy = pltpu.make_async_copy(lengths_hbm, lengths, sem)
    lengths_copy.start()
    count = scale_ref.shape[0]
    place = lax.axis_index("seq")
    width = left.shape[1]
    part = jnp.where(place < 2, 0, 1 - lax.rem(place, 2)) * width
    pieces = width // (2 * DH)

    def copies(sources):
        made = []
        for piece in range(pieces):
            for n, (source, target) in enumerate(zip(sources, (left, right))):
                column = pl.multiple_of(part + piece * 2 * DH, DH)
                made.append(
                    pltpu.make_async_copy(
                        source.at[:, pl.ds(column, 2 * DH)],
                        target.at[:, piece * 2 * DH : (piece + 1) * 2 * DH],
                        sems.at[n, piece],
                    )
                )
        return made

    def run(sources, total):
        made = copies(sources)
        for piece in range(pieces):
            made[2 * piece].wait()
            made[2 * piece + 1].wait()
            for h in (2 * piece, 2 * piece + 1):
                send_ref[h] = total(left[:, columns(h)], right[:, columns(h)])

    keys = place < 6

    @pl.when(keys)
    def _():
        for copy in copies((k_hbm, v_hbm)):
            copy.start()

    @pl.when(jnp.logical_not(keys))
    def _():
        for copy in copies((q_hbm, g_hbm)):
            copy.start()

    lengths_copy.wait()
    write_layout(lengths, place * count, scale_ref, first_ref)
    link_ref[...] = jnp.full(link_ref.shape, jnp.where(lengths[0] >= 2 * count, 1.0, 0.0), F32)

    @pl.when(keys)
    def _():
        start = first_ref[count - 1 : count]
        run((k_hbm, v_hbm), lambda k, v: key_values(k, v, start, 0))

    @pl.when(jnp.logical_not(keys))
    def _():
        run((q_hbm, g_hbm), lambda q, g: query_grads(q, g, scale_ref[...], first_ref[...], 0.0))


def states_kernel(q_hbm, k_hbm, v_hbm, g_hbm, scale_ref, first_ref, *refs):
    kv_ref, qg_ref, inner_kv_ref, inner_qg_ref, q_ref, k_ref, v_ref, g_ref, sems = refs
    count = q_ref.shape[0]
    chunks = count // ROWS
    steps = []
    for step in range(chunks):
        down, up = step * ROWS, (chunks - 1 - step) * ROWS
        made = []
        for n, (source, target, base) in enumerate(
            ((k_hbm, k_ref, down), (v_hbm, v_ref, down), (q_hbm, q_ref, up), (g_hbm, g_ref, up))
        ):
            rows = slice(base, base + ROWS)
            made.append(pltpu.make_async_copy(source.at[rows], target.at[rows], sems.at[n, step]))
        steps.append(made)
    for made in steps:
        for copy in made:
            copy.start()
    for step, made in enumerate(steps):
        for copy in made:
            copy.wait()
        down, up = step * ROWS, (chunks - 1 - step) * ROWS
        rows, back = slice(down, down + ROWS), slice(up, up + ROWS)
        start = first_ref[down + ROWS - 1 : down + ROWS]
        keep = jnp.where(start < down, 1.0, 0.0)
        up_keep = jnp.where(first_ref[up + ROWS - 1 : up + ROWS] < up, 1.0, 0.0)
        for h in range(kv_ref.shape[0]):
            cols = columns(h)
            kv = key_values(k_ref[rows, cols], v_ref[rows, cols], start, down)
            qg = query_grads(q_ref[back, cols], g_ref[back, cols], scale_ref[back], first_ref[back], up)
            if step:
                kv = inner_kv_ref[step - 1, h] * keep + kv
                qg = inner_qg_ref[chunks - 1 - step, h] * up_keep + qg
            if step < chunks - 1:
                inner_kv_ref[step, h] = kv
                inner_qg_ref[chunks - 2 - step, h] = qg
            else:
                kv_ref[h] = kv
                qg_ref[h] = qg


def part_columns(part, width, h):
    return pl.ds(pl.multiple_of(part * width + h * DH, DH), DH)


def local_kernel(pick, q_ref, k_ref, v_ref, g_ref, scale_ref, first_ref, tie_ref, a_ref, dq_ref, dk_ref, dv_ref):
    del tie_ref
    many = ROWS // DH
    count, width = a_ref.shape
    part = pick()
    row = lax.broadcasted_iota(jnp.int32, (ROWS, ROWS), 0)
    col = lax.broadcasted_iota(jnp.int32, (ROWS, ROWS), 1)
    causal = col <= row
    col = col.astype(F32)

    def chunk(c, _):
        base = pl.multiple_of(c * ROWS, ROWS)
        rows = pl.ds(base, ROWS)
        base = base.astype(F32)
        for h in range(width // DH):
            cols = part_columns(part, width, h)
            to = columns(h)
            q, g, k, v = q_ref[rows, cols], g_ref[rows, cols], k_ref[rows, cols], v_ref[rows, cols]
            scale = scale_ref[rows]
            start = jnp.concatenate([first_ref[rows] - base] * many, axis=1)
            scale_w = jnp.concatenate([scale] * many, axis=1)
            mask = (col >= start) & causal
            scores = jnp.where(mask, dot(q, k, NT), 0.0).astype(LOW)
            grads = jnp.where(mask, dot(g, v, NT) * scale_w, 0.0).astype(LOW)
            scaled = (scale * g.astype(F32)).astype(LOW)
            a_ref[rows, to] = scale * dot(scores, v, NN)
            dq_ref[rows, to] = dot(grads, k, NN)
            dk_ref[rows, to] = dot(grads, q, TN)
            dv_ref[rows, to] = dot(scores, scaled, TN)
        return 0

    lax.fori_loop(0, count // ROWS, chunk, 0)


def carried(rows, state, axis):
    both = jnp.concatenate(split(state), axis=axis)
    return dot(jnp.concatenate([rows, rows], axis=1), both, NT if axis else NN)


class Pair:
    def __init__(self, forward, part, rows, inner, layout, parts, state, kept, outs, sems):
        self.forward, self.part, self.rows, self.inner = forward, part, rows, inner
        self.layout, self.parts, self.state, self.kept = layout, parts, state, kept
        self.count, self.width = kept[0].shape
        self.copies = []
        column = pl.ds(pl.multiple_of(part * self.width, DH), self.width)
        for c in range(self.count // ROWS):
            span = slice(c * ROWS, (c + 1) * ROWS)
            for n in range(2):
                self.copies.append(pltpu.make_async_copy(kept[n].at[span], outs[n].at[span, column], sems.at[n, c]))

    def chunk(self, c):
        scale_ref, first_ref = self.layout
        heads = self.width // DH
        base = c * ROWS
        rows = slice(base, base + ROWS)
        if self.forward:
            factor = jnp.where(first_ref[rows] < base, scale_ref[rows], 0.0)
        else:
            tail = row_index(ROWS, base) >= first_ref[base + ROWS - 1 : base + ROWS]
        for h in range(heads):
            cols = part_columns(self.part, self.width, h)
            to = columns(h)
            state = self.state[h]
            if self.forward and c:
                keep = jnp.where(first_ref[base - 1 : base] < 0, 1.0, 0.0)
                state = state * keep + self.inner[c - 1, self.part * heads + h]
            if not self.forward and base + ROWS < self.count:
                keep = jnp.where(first_ref[self.count - 1 : self.count] < base + ROWS, 1.0, 0.0)
                state = state * keep + self.inner[c, self.part * heads + h]
            for n, axis in enumerate((0, 1) if self.forward else (1, 0)):
                more = carried(self.rows[n][rows, cols], state, axis)
                more = factor * more if self.forward else jnp.where(tail, more, 0.0)
                self.kept[n][rows, to] = (self.parts[n][rows, to] + more).astype(LOW)
        for copy in self.copies[2 * c : 2 * c + 2]:
            copy.start()

    def run(self):
        for c in range(self.count // ROWS):
            self.chunk(c)

    def wait(self):
        for copy in self.copies:
            copy.wait()


def final_kernel(body, inputs, scratch, *refs):
    body(refs[:inputs], refs[-scratch - 4 : -scratch], refs[-scratch:])


IN_VMEM = pl.BlockSpec(memory_space=pltpu.VMEM)
IN_HBM = pl.BlockSpec(memory_space=pltpu.HBM)
PARAMS = pltpu.CompilerParams(vmem_limit_bytes=VMEM_LIMIT)


def call(kernel, name, out_shape, in_specs, out_specs, scratch=(), aliases=None):
    return pl.pallas_call(
        kernel,
        out_shape=out_shape,
        in_specs=in_specs,
        out_specs=out_specs,
        scratch_shapes=scratch,
        input_output_aliases=aliases or {},
        compiler_params=PARAMS,
        name=name,
    )


def sums_shape(heads, *lead):
    return jax.ShapeDtypeStruct((*lead, heads, DH, DH), F32)


def first_send(arrays, lengths, heads):
    count = arrays[0].shape[0]
    width = heads * DH
    row = jax.ShapeDtypeStruct((count, DH), F32)
    return call(
        first_kernel,
        "first",
        [sums_shape(heads), row, row, jax.ShapeDtypeStruct((DH, DH), F32)],
        [IN_HBM] * 5,
        [IN_VMEM] * 4,
        [pltpu.SMEM(lengths.shape, jnp.int32)]
        + [pltpu.VMEM((count, width), LOW)] * 2
        + [pltpu.SemaphoreType.DMA((2, heads // 2)), pltpu.SemaphoreType.DMA(())],
    )(lengths, *arrays)


def states(arrays, layout):
    count, width = arrays[0].shape
    heads = width // DH
    chunks = count // ROWS
    outs = call(
        states_kernel,
        "states",
        [sums_shape(heads)] * 2
        + [sums_shape(heads, chunks - 1)] * 2
        + [jax.ShapeDtypeStruct((count, width), LOW)] * 4,
        [IN_HBM] * 4 + [IN_VMEM] * 2,
        [IN_VMEM] * 8,
        [pltpu.SemaphoreType.DMA((4, chunks))],
    )(*arrays, *layout)
    return outs[:4], outs[4:]


def local(arrays, layout, heads, pick, tie):
    count = arrays[0].shape[0]
    shape = jax.ShapeDtypeStruct((count, heads * DH), F32)
    return call(
        functools.partial(local_kernel, pick),
        "local",
        [shape] * 4,
        [IN_VMEM] * 6 + [pl.BlockSpec(memory_space=pl.ANY)],
        [IN_VMEM] * 4,
    )(*arrays, *layout, tie)


def final(body, inputs, shape, width, pairs, outs=None):
    count = shape[0]
    chunks, heads = count // ROWS, width // DH
    extra = tuple(outs or ())
    scratch = [pltpu.VMEM((heads, DH, DH), F32)] * pairs
    scratch += [pltpu.VMEM((count, width), LOW)] * (2 * pairs)
    scratch += [pltpu.SemaphoreType.DMA((2, chunks))] * pairs
    return call(
        functools.partial(final_kernel, body, len(inputs), len(scratch)),
        "final",
        [jax.ShapeDtypeStruct(shape, LOW)] * 4,
        [IN_VMEM] * len(inputs) + [IN_HBM] * len(extra),
        [IN_HBM] * 4,
        scratch,
        {len(inputs) + i: i for i in range(len(extra))},
    )(*inputs, *extra)


def make_pairs(scratch, pairs):
    states, kept, sems = scratch[:pairs], scratch[pairs : 3 * pairs], scratch[3 * pairs :]
    return [(states[n], kept[2 * n : 2 * n + 2], sems[n]) for n in range(pairs)]


PAIRS = [(d, d ^ 1) for d in range(8)]
PAIRS_2 = [(0, 1), (1, 0), (4, 5), (5, 4)]
UP_1 = [(0, 2), (2, 4), (3, 5)]
UP_2 = [(0, 2), (4, 6), (5, 7)]
DOWN_1 = [(2, 0), (6, 4), (7, 5)]
DOWN_2 = [(2, 0), (4, 2), (5, 3)]


def put(ref, *cases):
    place = lax.axis_index("seq")
    for devices, value in cases:
        hit = functools.reduce(jnp.logical_or, [place == d for d in devices])

        @pl.when(hit)
        def _():
            ref[...] = value()


def permute(value, pairs):
    return lax.ppermute(value, "seq", pairs)


def select(kernel, name, outs, heads, *taken):
    return call(kernel, name, [sums_shape(heads)] * outs, [IN_VMEM] * len(taken), [IN_VMEM] * outs)(*taken)


def own():
    return lax.rem(lax.axis_index("seq"), 2)


def other():
    return 1 - own()


def on_eight(arrays, lengths):
    count, width = arrays[0].shape
    heads = width // DH
    half = heads // 2
    low, high = slice(0, half), slice(half, heads)

    def select_0(kv, qg, send):
        put(
            send,
            ((0, 1, 6), lambda: kv[high]),
            ((2,), lambda: kv[low]),
            ((3, 5), lambda: qg[low]),
            ((4, 7), lambda: qg[high]),
        )

    def select_1(x0, link, kv, qg, up, down):
        put(
            up,
            ((0,), lambda: x0[...] + link[...] * kv[low]),
            ((2, 4), lambda: x0[...] + kv[low]),
            ((3, 5), lambda: x0[...] + kv[high]),
        )
        put(
            down,
            ((2,), lambda: qg[high]),
            ((6,), lambda: x0[...] + qg[low]),
            ((7,), lambda: x0[...] + qg[high]),
        )

    def select_2(x0, x1, link, up1, down1, kv, qg, up, down, send):
        put(
            up,
            ((0,), lambda: x1[...] + link[...] * kv[high]),
            ((4,), lambda: up1[...] + (x0[...] + kv[low])),
            ((5,), lambda: up1[...] + (x0[...] + kv[high])),
        )
        put(
            down,
            ((2,), lambda: qg[low]),
            ((4,), lambda: down1[...] + (x1[...] + qg[low])),
            ((5,), lambda: down1[...] + (x1[...] + qg[high])),
        )
        put(
            send,
            ((0,), lambda: down1[...]),
            ((1,), lambda: qg[low]),
            ((4,), lambda: up1[...] + kv[low]),
            ((5,), lambda: up1[...]),
        )

    def select_3(down1, up2, down2, kv, qg, send):
        put(
            send,
            ((0, 2), lambda: down2[...]),
            ((1,), lambda: qg[high]),
            ((3,), lambda: down2[...] + qg[high]),
            ((4,), lambda: down1[...]),
            ((5,), lambda: down1[...] + qg[high]),
            ((6,), lambda: up2[...] + kv[low]),
            ((7,), lambda: up2[...]),
        )

    def pair(forward, part, taken, outs, made):
        rows, inner, layout, parts = taken
        state, kept, sems = made
        q, k, v, g = rows
        if forward:
            return Pair(True, part, (q, g), inner[0], layout, parts[:2], state, kept, outs[:2], sems)
        return Pair(False, part, (v, k), inner[1], layout, parts[2:], state, kept, outs[2:], sems)

    def final_1(inputs, outs, scratch):
        rows, inner, layout, mine, others = inputs[:4], inputs[4:6], inputs[6:8], inputs[8:12], inputs[12:16]
        link, x0, x1, x2, up1, down1, up2, down2 = inputs[16:]
        made = make_pairs(scratch, 3)
        kv, qg, more = (m[0] for m in made)
        put(
            kv,
            ((0,), lambda: jnp.zeros_like(kv)),
            ((1,), lambda: x1[...]),
            ((2, 4), lambda: up1[...]),
            ((3,), lambda: x0[...]),
            ((5,), lambda: up1[...] + x0[...]),
            ((6,), lambda: up2[...]),
            ((7,), lambda: up2[...] + x1[...]),
        )
        put(
            qg,
            ((0,), lambda: x2[...] + link[...] * down2[...]),
            ((1,), lambda: x2[...]),
            ((2,), lambda: x1[...] + down2[...]),
            ((3,), lambda: down2[...]),
            ((4,), lambda: x1[...] + down1[...]),
            ((5,), lambda: down1[...]),
            ((6,), lambda: x0[...]),
            ((7,), lambda: jnp.zeros_like(qg)),
        )
        put(
            more,
            ((0, 7), lambda: jnp.zeros_like(more)),
            ((1,), lambda: x0[...]),
            ((2,), lambda: up2[...]),
            ((3, 6), lambda: x1[...]),
            ((4, 5), lambda: x2[...]),
        )
        ahead = [pair(f, other(), (rows, inner, layout, others), outs, made[2]) for f in (True, False)]
        pairs = [pair(f, own(), (rows, inner, layout, mine), outs, m) for f, m in zip((True, False), made)]
        forward = lax.axis_index("seq") < 6

        @pl.when(forward)
        def _():
            ahead[0].run()

        @pl.when(jnp.logical_not(forward))
        def _():
            ahead[1].run()

        for p in pairs:
            p.run()

        @pl.when(forward)
        def _():
            ahead[0].wait()

        @pl.when(jnp.logical_not(forward))
        def _():
            ahead[1].wait()

        for p in pairs:
            p.wait()

    def final_2(inputs, outs, scratch):
        rows, inner, layout, others = inputs[:4], inputs[4:6], inputs[6:8], inputs[8:12]
        link, x3, down1 = inputs[12:]
        (made,) = make_pairs(scratch, 1)
        state = made[0]
        put(
            state,
            ((0,), lambda: x3[...] + link[...] * down1[...]),
            ((1, 2, 3, 4, 5, 6, 7), lambda: x3[...]),
        )
        forward = lax.axis_index("seq") >= 6

        @pl.when(forward)
        def _():
            p = pair(True, other(), (rows, inner, layout, others), outs, made)
            p.run()
            p.wait()

        @pl.when(jnp.logical_not(forward))
        def _():
            p = pair(False, other(), (rows, inner, layout, others), outs, made)
            p.run()
            p.wait()

    shape, part_width = (count, width), half * DH
    send, *layout, link = first_send(arrays, lengths, half)
    x0 = permute(send, PAIRS)
    (kv, qg, *inner), arrays = states(arrays, layout)
    (send,) = select(select_0, "select0", 1, half, kv, qg)
    x1 = permute(send, PAIRS)
    x0, kv, qg = lax.optimization_barrier((x0, kv, qg))
    up, down = select(select_1, "select1", 2, half, x0, link, kv, qg)
    up1, down1 = permute(up, UP_1), permute(down, DOWN_1)
    mine = local(arrays, layout, half, own, up)
    x1, up1, down1, *mine = lax.optimization_barrier((x1, up1, down1, *mine))
    up, down, send = select(select_2, "select2", 3, half, x0, x1, link, up1, down1, kv, qg)
    up2, down2 = permute(up, UP_2), permute(down, DOWN_2)
    x2 = permute(send, PAIRS_2)
    others = local(arrays, layout, half, other, send)
    up2, down2, *others = lax.optimization_barrier((up2, down2, *others))
    (send,) = select(select_3, "select3", 1, half, down1, up2, down2, kv, qg)
    x3 = permute(send, PAIRS)
    fixed = (*arrays, *inner, *layout)
    outs = final(
        final_1, (*fixed, *mine, *others, link, x0, x1, x2, up1, down1, up2, down2), shape, part_width, 3
    )
    x3, *outs = lax.optimization_barrier((x3, *outs))
    return tuple(final(final_2, (*fixed, *others, link, x3, down1), shape, part_width, 1, outs))


def on_any(arrays, lengths):
    count, width = arrays[0].shape
    heads = width // DH
    _, *layout, _ = first_send(arrays, lengths, heads // 2)
    (kv, qg, *inner), arrays = states(arrays, layout)
    parts = local(arrays, layout, heads, lambda: jnp.int32(0), kv)
    starts_here = (layout[1][count - 1, 0] >= 0).astype(F32)
    kv_all, qg_all, start_all = lax.all_gather((kv, qg, starts_here), "seq")
    place = lax.axis_index("seq")
    devices = lax.axis_size("seq")
    order = jnp.arange(devices)
    last_start = jnp.max(jnp.where((order < place) & (start_all > 0.5), order, 0))
    next_start = jnp.min(jnp.where((order > place) & (start_all > 0.5), order, devices))

    def total(pick, values):
        return jnp.sum(jnp.where(pick[:, None, None, None], values, 0.0), axis=0)

    before = total((order < place) & (order >= last_start), kv_all)
    after = total((order > place) & (order <= next_start), qg_all)

    def body(inputs, outs, scratch):
        q, k, v, g, inner_kv, inner_qg, scale, first, a, dq, dk, dv, kv_ref, qg_ref = inputs
        made = make_pairs(scratch, 2)
        zero = jnp.int32(0)
        for p in (
            Pair(True, zero, (q, g), inner_kv, (scale, first), (a, dq), kv_ref, made[0][1], outs[:2], made[0][2]),
            Pair(False, zero, (v, k), inner_qg, (scale, first), (dk, dv), qg_ref, made[1][1], outs[2:], made[1][2]),
        ):
            p.run()
            p.wait()

    return tuple(final(body, (*arrays, *inner, *layout, *parts, before, after), (count, width), width, 2))


def per_device(query_rows, key_rows, value_rows, grad_out, doc_lengths):
    *arrays, doc_lengths = (
        pltpu.with_memory_space_constraint(a, pltpu.HBM)
        for a in (query_rows, key_rows, value_rows, grad_out, doc_lengths)
    )
    if lax.axis_size("seq") == 8:
        return on_eight(arrays, doc_lengths)
    return on_any(arrays, doc_lengths)


def solution(mesh):
    placed = P("seq", "head")
    return jax.shard_map(
        per_device,
        mesh=mesh,
        in_specs=(placed, placed, placed, placed, P()),
        out_specs=(placed, placed, placed, placed),
        check_vma=False,
    )
```

```python
import functools

import jax
import jax.numpy as jnp
from jax import lax
from jax.experimental import pallas as pl
from jax.experimental.pallas import tpu as pltpu
from jax.sharding import PartitionSpec as P

DH = 128
ROWS = 256
VMEM_LIMIT = 16 << 20
F32 = jnp.float32
LOW = jnp.bfloat16

NT = (((1,), (1,)), ((), ()))
TN = (((0,), (0,)), ((), ()))
NN = (((1,), (0,)), ((), ()))


def dot(a, b, dims):
    return lax.dot_general(a, b, dims, preferred_element_type=F32)


def split(a):
    high = a.astype(LOW)
    return high, (a - high.astype(F32)).astype(LOW)


def write_layout(lengths, offset, scale_ref, first_ref):
    count = scale_ref.shape[0]
    tiles = count // DH
    shape = (tiles, DH)
    row = lax.broadcasted_iota(jnp.int32, shape, 0) * DH + lax.broadcasted_iota(jnp.int32, shape, 1) + offset
    first = jnp.zeros(shape, jnp.int32)
    start = jnp.int32(0)
    for j in range(lengths.shape[0]):
        first = jnp.where(row >= start, start, first)
        start = start + lengths[j]
    scale = 1.0 / jnp.sqrt((row - first + 1).astype(F32) * DH)
    first = (first - offset).astype(F32)
    for t in range(tiles):
        rows = slice(t * DH, (t + 1) * DH)
        scale_ref[rows] = jnp.broadcast_to(scale[t : t + 1], (DH, DH)).T
        first_ref[rows] = jnp.broadcast_to(first[t : t + 1], (DH, DH)).T


def row_index(rows, base):
    return (lax.broadcasted_iota(jnp.int32, (rows, DH), 0) + base).astype(F32)


def key_values(k, v, start, base):
    tail = jnp.where(row_index(k.shape[0], base) >= start, k, jnp.zeros((), LOW))
    return dot(tail, v, TN)


def query_grads(q, g, scale, first, base):
    scaled = jnp.where(first < base, scale * g.astype(F32), 0.0)
    both = dot(q, jnp.concatenate(split(scaled), axis=1), TN)
    return both[:, :DH] + both[:, DH:]


def columns(h):
    return slice(h * DH, (h + 1) * DH)


def first_kernel(
    lengths_hbm, q_hbm, k_hbm, v_hbm, g_hbm, send_ref, scale_ref, first_ref, link_ref, lengths, left, right, sems, sem
):
    lengths_copy = pltpu.make_async_copy(lengths_hbm, lengths, sem)
    lengths_copy.start()
    count = scale_ref.shape[0]
    place = lax.axis_index("seq")
    width = left.shape[1]
    part = jnp.where(place < 2, 0, 1 - lax.rem(place, 2)) * width
    pieces = width // (2 * DH)

    def copies(sources):
        made = []
        for piece in range(pieces):
            for n, (source, target) in enumerate(zip(sources, (left, right))):
                column = pl.multiple_of(part + piece * 2 * DH, DH)
                made.append(
                    pltpu.make_async_copy(
                        source.at[:, pl.ds(column, 2 * DH)],
                        target.at[:, piece * 2 * DH : (piece + 1) * 2 * DH],
                        sems.at[n, piece],
                    )
                )
        return made

    def run(sources, total):
        made = copies(sources)
        for piece in range(pieces):
            made[2 * piece].wait()
            made[2 * piece + 1].wait()
            for h in (2 * piece, 2 * piece + 1):
                send_ref[h] = total(left[:, columns(h)], right[:, columns(h)])

    keys = place < 6

    @pl.when(keys)
    def _():
        for copy in copies((k_hbm, v_hbm)):
            copy.start()

    @pl.when(jnp.logical_not(keys))
    def _():
        for copy in copies((q_hbm, g_hbm)):
            copy.start()

    lengths_copy.wait()
    write_layout(lengths, place * count, scale_ref, first_ref)
    link_ref[...] = jnp.full(link_ref.shape, jnp.where(lengths[0] >= 2 * count, 1.0, 0.0), F32)

    @pl.when(keys)
    def _():
        start = first_ref[count - 1 : count]
        run((k_hbm, v_hbm), lambda k, v: key_values(k, v, start, 0))

    @pl.when(jnp.logical_not(keys))
    def _():
        run((q_hbm, g_hbm), lambda q, g: query_grads(q, g, scale_ref[...], first_ref[...], 0.0))


def states_kernel(q_hbm, k_hbm, v_hbm, g_hbm, scale_ref, first_ref, *refs):
    kv_ref, qg_ref, inner_kv_ref, inner_qg_ref, q_ref, k_ref, v_ref, g_ref, sems = refs
    count = q_ref.shape[0]
    chunks = count // ROWS
    steps = []
    for step in range(chunks):
        down, up = step * ROWS, (chunks - 1 - step) * ROWS
        made = []
        for n, (source, target, base) in enumerate(
            ((k_hbm, k_ref, down), (v_hbm, v_ref, down), (q_hbm, q_ref, up), (g_hbm, g_ref, up))
        ):
            rows = slice(base, base + ROWS)
            made.append(pltpu.make_async_copy(source.at[rows], target.at[rows], sems.at[n, step]))
        steps.append(made)
    for made in steps:
        for copy in made:
            copy.start()
    for step, made in enumerate(steps):
        for copy in made:
            copy.wait()
        down, up = step * ROWS, (chunks - 1 - step) * ROWS
        rows, back = slice(down, down + ROWS), slice(up, up + ROWS)
        start = first_ref[down + ROWS - 1 : down + ROWS]
        keep = jnp.where(start < down, 1.0, 0.0)
        up_keep = jnp.where(first_ref[up + ROWS - 1 : up + ROWS] < up, 1.0, 0.0)
        for h in range(kv_ref.shape[0]):
            cols = columns(h)
            kv = key_values(k_ref[rows, cols], v_ref[rows, cols], start, down)
            qg = query_grads(q_ref[back, cols], g_ref[back, cols], scale_ref[back], first_ref[back], up)
            if step:
                kv = inner_kv_ref[step - 1, h] * keep + kv
                qg = inner_qg_ref[chunks - 1 - step, h] * up_keep + qg
            if step < chunks - 1:
                inner_kv_ref[step, h] = kv
                inner_qg_ref[chunks - 2 - step, h] = qg
            else:
                kv_ref[h] = kv
                qg_ref[h] = qg


def part_columns(part, width, h):
    return pl.ds(pl.multiple_of(part * width + h * DH, DH), DH)


def local_kernel(pick, q_ref, k_ref, v_ref, g_ref, scale_ref, first_ref, tie_ref, a_ref, dq_ref, dk_ref, dv_ref):
    del tie_ref
    many = ROWS // DH
    count, width = a_ref.shape
    part = pick()
    row = lax.broadcasted_iota(jnp.int32, (ROWS, ROWS), 0)
    col = lax.broadcasted_iota(jnp.int32, (ROWS, ROWS), 1)
    causal = col <= row
    col = col.astype(F32)

    def chunk(c, _):
        base = pl.multiple_of(c * ROWS, ROWS)
        rows = pl.ds(base, ROWS)
        base = base.astype(F32)
        for h in range(width // DH):
            cols = part_columns(part, width, h)
            to = columns(h)
            q, g, k, v = q_ref[rows, cols], g_ref[rows, cols], k_ref[rows, cols], v_ref[rows, cols]
            scale = scale_ref[rows]
            start = jnp.concatenate([first_ref[rows] - base] * many, axis=1)
            scale_w = jnp.concatenate([scale] * many, axis=1)
            mask = (col >= start) & causal
            scores = jnp.where(mask, dot(q, k, NT), 0.0).astype(LOW)
            grads = jnp.where(mask, dot(g, v, NT) * scale_w, 0.0).astype(LOW)
            scaled = (scale * g.astype(F32)).astype(LOW)
            a_ref[rows, to] = scale * dot(scores, v, NN)
            dq_ref[rows, to] = dot(grads, k, NN)
            dk_ref[rows, to] = dot(grads, q, TN)
            dv_ref[rows, to] = dot(scores, scaled, TN)
        return 0

    lax.fori_loop(0, count // ROWS, chunk, 0)


def carried(rows, state, axis):
    both = jnp.concatenate(split(state), axis=axis)
    return dot(jnp.concatenate([rows, rows], axis=1), both, NT if axis else NN)


class Pair:
    def __init__(self, forward, part, rows, inner, layout, parts, state, kept, outs, sems):
        self.forward, self.part, self.rows, self.inner = forward, part, rows, inner
        self.layout, self.parts, self.state, self.kept = layout, parts, state, kept
        self.count, self.width = kept[0].shape
        self.copies = []
        column = pl.ds(pl.multiple_of(part * self.width, DH), self.width)
        for c in range(self.count // ROWS):
            span = slice(c * ROWS, (c + 1) * ROWS)
            for n in range(2):
                self.copies.append(pltpu.make_async_copy(kept[n].at[span], outs[n].at[span, column], sems.at[n, c]))

    def chunk(self, c):
        scale_ref, first_ref = self.layout
        heads = self.width // DH
        base = c * ROWS
        rows = slice(base, base + ROWS)
        if self.forward:
            factor = jnp.where(first_ref[rows] < base, scale_ref[rows], 0.0)
        else:
            tail = row_index(ROWS, base) >= first_ref[base + ROWS - 1 : base + ROWS]
        for h in range(heads):
            cols = part_columns(self.part, self.width, h)
            to = columns(h)
            state = self.state[h]
            if self.forward and c:
                keep = jnp.where(first_ref[base - 1 : base] < 0, 1.0, 0.0)
                state = state * keep + self.inner[c - 1, self.part * heads + h]
            if not self.forward and base + ROWS < self.count:
                keep = jnp.where(first_ref[self.count - 1 : self.count] < base + ROWS, 1.0, 0.0)
                state = state * keep + self.inner[c, self.part * heads + h]
            for n, axis in enumerate((0, 1) if self.forward else (1, 0)):
                more = carried(self.rows[n][rows, cols], state, axis)
                more = factor * more if self.forward else jnp.where(tail, more, 0.0)
                self.kept[n][rows, to] = (self.parts[n][rows, to] + more).astype(LOW)
        for copy in self.copies[2 * c : 2 * c + 2]:
            copy.start()

    def run(self):
        for c in range(self.count // ROWS):
            self.chunk(c)

    def wait(self):
        for copy in self.copies:
            copy.wait()


def final_kernel(body, inputs, scratch, *refs):
    body(refs[:inputs], refs[-scratch - 4 : -scratch], refs[-scratch:])


IN_VMEM = pl.BlockSpec(memory_space=pltpu.VMEM)
IN_HBM = pl.BlockSpec(memory_space=pltpu.HBM)
PARAMS = pltpu.CompilerParams(vmem_limit_bytes=VMEM_LIMIT)


def call(kernel, name, out_shape, in_specs, out_specs, scratch=(), aliases=None):
    return pl.pallas_call(
        kernel,
        out_shape=out_shape,
        in_specs=in_specs,
        out_specs=out_specs,
        scratch_shapes=scratch,
        input_output_aliases=aliases or {},
        compiler_params=PARAMS,
        name=name,
    )


def sums_shape(heads, *lead):
    return jax.ShapeDtypeStruct((*lead, heads, DH, DH), F32)


def first_send(arrays, lengths, heads):
    count = arrays[0].shape[0]
    width = heads * DH
    row = jax.ShapeDtypeStruct((count, DH), F32)
    return call(
        first_kernel,
        "first",
        [sums_shape(heads), row, row, jax.ShapeDtypeStruct((DH, DH), F32)],
        [IN_HBM] * 5,
        [IN_VMEM] * 4,
        [pltpu.SMEM(lengths.shape, jnp.int32)]
        + [pltpu.VMEM((count, width), LOW)] * 2
        + [pltpu.SemaphoreType.DMA((2, heads // 2)), pltpu.SemaphoreType.DMA(())],
    )(lengths, *arrays)


def states(arrays, layout):
    count, width = arrays[0].shape
    heads = width // DH
    chunks = count // ROWS
    outs = call(
        states_kernel,
        "states",
        [sums_shape(heads)] * 2
        + [sums_shape(heads, chunks - 1)] * 2
        + [jax.ShapeDtypeStruct((count, width), LOW)] * 4,
        [IN_HBM] * 4 + [IN_VMEM] * 2,
        [IN_VMEM] * 8,
        [pltpu.SemaphoreType.DMA((4, chunks))],
    )(*arrays, *layout)
    return outs[:4], outs[4:]


def local(arrays, layout, heads, pick, tie):
    count = arrays[0].shape[0]
    shape = jax.ShapeDtypeStruct((count, heads * DH), F32)
    return call(
        functools.partial(local_kernel, pick),
        "local",
        [shape] * 4,
        [IN_VMEM] * 6 + [pl.BlockSpec(memory_space=pl.ANY)],
        [IN_VMEM] * 4,
    )(*arrays, *layout, tie)


def final(body, inputs, shape, width, pairs, outs=None):
    count = shape[0]
    chunks, heads = count // ROWS, width // DH
    extra = tuple(outs or ())
    scratch = [pltpu.VMEM((heads, DH, DH), F32)] * pairs
    scratch += [pltpu.VMEM((count, width), LOW)] * (2 * pairs)
    scratch += [pltpu.SemaphoreType.DMA((2, chunks))] * pairs
    return call(
        functools.partial(final_kernel, body, len(inputs), len(scratch)),
        "final",
        [jax.ShapeDtypeStruct(shape, LOW)] * 4,
        [IN_VMEM] * len(inputs) + [IN_HBM] * len(extra),
        [IN_HBM] * 4,
        scratch,
        {len(inputs) + i: i for i in range(len(extra))},
    )(*inputs, *extra)


def make_pairs(scratch, pairs):
    states, kept, sems = scratch[:pairs], scratch[pairs : 3 * pairs], scratch[3 * pairs :]
    return [(states[n], kept[2 * n : 2 * n + 2], sems[n]) for n in range(pairs)]


PAIRS = [(d, d ^ 1) for d in range(8)]
PAIRS_2 = [(0, 1), (1, 0), (4, 5), (5, 4)]
UP_1 = [(2, 4), (3, 5)]
UP_2 = [(0, 2), (2, 0), (4, 6), (5, 7)]
DOWN_1 = [(0, 2), (2, 0), (6, 4), (7, 5)]
DOWN_2 = [(4, 2), (5, 3)]


def put(ref, *cases):
    place = lax.axis_index("seq")
    for devices, value in cases:
        hit = functools.reduce(jnp.logical_or, [place == d for d in devices])

        @pl.when(hit)
        def _():
            ref[...] = value()


def permute(value, pairs):
    return lax.ppermute(value, "seq", pairs)


def select(kernel, name, outs, heads, *taken):
    return call(kernel, name, [sums_shape(heads)] * outs, [IN_VMEM] * len(taken), [IN_VMEM] * outs)(*taken)


def own():
    return lax.rem(lax.axis_index("seq"), 2)


def other():
    return 1 - own()


def on_eight(arrays, lengths):
    count, width = arrays[0].shape
    heads = width // DH
    half = heads // 2
    low, high = slice(0, half), slice(half, heads)

    def select_0(kv, qg, send):
        put(
            send,
            ((0, 1, 6), lambda: kv[high]),
            ((2,), lambda: kv[low]),
            ((3, 5), lambda: qg[low]),
            ((4, 7), lambda: qg[high]),
        )

    def select_1(x0, link, kv, qg, up, down):
        put(
            up,
            ((2, 4), lambda: x0[...] + kv[low]),
            ((3, 5), lambda: x0[...] + kv[high]),
        )
        put(
            down,
            ((0,), lambda: x0[...] + link[...] * kv[low]),
            ((2,), lambda: qg[high]),
            ((6,), lambda: x0[...] + qg[low]),
            ((7,), lambda: x0[...] + qg[high]),
        )

    def select_2(x0, x1, link, up1, down1, kv, qg, up, down, send):
        put(
            up,
            ((0,), lambda: x1[...] + link[...] * kv[high]),
            ((2,), lambda: qg[low]),
            ((4,), lambda: up1[...] + (x0[...] + kv[low])),
            ((5,), lambda: up1[...] + (x0[...] + kv[high])),
        )
        put(
            down,
            ((4,), lambda: down1[...] + (x1[...] + qg[low])),
            ((5,), lambda: down1[...] + (x1[...] + qg[high])),
        )
        put(
            send,
            ((0,), lambda: down1[...]),
            ((1,), lambda: qg[low]),
            ((4,), lambda: up1[...] + kv[low]),
            ((5,), lambda: up1[...]),
        )

    def select_3(down1, up2, down2, kv, qg, send):
        put(
            send,
            ((0,), lambda: up2[...]),
            ((2,), lambda: down2[...]),
            ((1,), lambda: qg[high]),
            ((3,), lambda: down2[...] + qg[high]),
            ((4,), lambda: down1[...]),
            ((5,), lambda: down1[...] + qg[high]),
            ((6,), lambda: up2[...] + kv[low]),
            ((7,), lambda: up2[...]),
        )

    def pair(forward, part, taken, outs, made):
        rows, inner, layout, parts = taken
        state, kept, sems = made
        q, k, v, g = rows
        if forward:
            return Pair(True, part, (q, g), inner[0], layout, parts[:2], state, kept, outs[:2], sems)
        return Pair(False, part, (v, k), inner[1], layout, parts[2:], state, kept, outs[2:], sems)

    def final_1(inputs, outs, scratch):
        rows, inner, layout, mine, others = inputs[:4], inputs[4:6], inputs[6:8], inputs[8:12], inputs[12:16]
        link, x0, x1, x2, up1, down1, up2, down2 = inputs[16:]
        made = make_pairs(scratch, 3)
        kv, qg, more = (m[0] for m in made)
        put(
            kv,
            ((0,), lambda: jnp.zeros_like(kv)),
            ((1,), lambda: x1[...]),
            ((2,), lambda: down1[...]),
            ((4,), lambda: up1[...]),
            ((3,), lambda: x0[...]),
            ((5,), lambda: up1[...] + x0[...]),
            ((6,), lambda: up2[...]),
            ((7,), lambda: up2[...] + x1[...]),
        )
        put(
            qg,
            ((0,), lambda: x2[...] + link[...] * up2[...]),
            ((1,), lambda: x2[...]),
            ((2,), lambda: x1[...] + down2[...]),
            ((3,), lambda: down2[...]),
            ((4,), lambda: x1[...] + down1[...]),
            ((5,), lambda: down1[...]),
            ((6,), lambda: x0[...]),
            ((7,), lambda: jnp.zeros_like(qg)),
        )
        put(
            more,
            ((0, 7), lambda: jnp.zeros_like(more)),
            ((1,), lambda: x0[...]),
            ((2,), lambda: up2[...]),
            ((3, 6), lambda: x1[...]),
            ((4, 5), lambda: x2[...]),
        )
        ahead = [pair(f, other(), (rows, inner, layout, others), outs, made[2]) for f in (True, False)]
        pairs = [pair(f, own(), (rows, inner, layout, mine), outs, m) for f, m in zip((True, False), made)]
        forward = lax.axis_index("seq") < 6

        @pl.when(forward)
        def _():
            ahead[0].run()

        @pl.when(jnp.logical_not(forward))
        def _():
            ahead[1].run()

        for p in pairs:
            p.run()

        @pl.when(forward)
        def _():
            ahead[0].wait()

        @pl.when(jnp.logical_not(forward))
        def _():
            ahead[1].wait()

        for p in pairs:
            p.wait()

    def final_2(inputs, outs, scratch):
        rows, inner, layout, others = inputs[:4], inputs[4:6], inputs[6:8], inputs[8:12]
        link, x3, down1 = inputs[12:]
        (made,) = make_pairs(scratch, 1)
        state = made[0]
        put(
            state,
            ((0,), lambda: x3[...] + link[...] * down1[...]),
            ((1, 2, 3, 4, 5, 6, 7), lambda: x3[...]),
        )
        forward = lax.axis_index("seq") >= 6

        @pl.when(forward)
        def _():
            p = pair(True, other(), (rows, inner, layout, others), outs, made)
            p.run()
            p.wait()

        @pl.when(jnp.logical_not(forward))
        def _():
            p = pair(False, other(), (rows, inner, layout, others), outs, made)
            p.run()
            p.wait()

    shape, part_width = (count, width), half * DH
    send, *layout, link = first_send(arrays, lengths, half)
    x0 = permute(send, PAIRS)
    (kv, qg, *inner), arrays = states(arrays, layout)
    (send,) = select(select_0, "select0", 1, half, kv, qg)
    x1 = permute(send, PAIRS)
    x0, kv, qg = lax.optimization_barrier((x0, kv, qg))
    up, down = select(select_1, "select1", 2, half, x0, link, kv, qg)
    up1, down1 = permute(up, UP_1), permute(down, DOWN_1)
    mine = local(arrays, layout, half, own, up)
    x1, up1, down1, *mine = lax.optimization_barrier((x1, up1, down1, *mine))
    up, down, send = select(select_2, "select2", 3, half, x0, x1, link, up1, down1, kv, qg)
    up2, down2 = permute(up, UP_2), permute(down, DOWN_2)
    x2 = permute(send, PAIRS_2)
    others = local(arrays, layout, half, other, send)
    up2, down2, *others = lax.optimization_barrier((up2, down2, *others))
    (send,) = select(select_3, "select3", 1, half, down1, up2, down2, kv, qg)
    x3 = permute(send, PAIRS)
    fixed = (*arrays, *inner, *layout)
    outs = final(
        final_1, (*fixed, *mine, *others, link, x0, x1, x2, up1, down1, up2, down2), shape, part_width, 3
    )
    x3, *outs = lax.optimization_barrier((x3, *outs))
    return tuple(final(final_2, (*fixed, *others, link, x3, down1), shape, part_width, 1, outs))


def on_any(arrays, lengths):
    count, width = arrays[0].shape
    heads = width // DH
    _, *layout, _ = first_send(arrays, lengths, heads // 2)
    (kv, qg, *inner), arrays = states(arrays, layout)
    parts = local(arrays, layout, heads, lambda: jnp.int32(0), kv)
    starts_here = (layout[1][count - 1, 0] >= 0).astype(F32)
    kv_all, qg_all, start_all = lax.all_gather((kv, qg, starts_here), "seq")
    place = lax.axis_index("seq")
    devices = lax.axis_size("seq")
    order = jnp.arange(devices)
    last_start = jnp.max(jnp.where((order < place) & (start_all > 0.5), order, 0))
    next_start = jnp.min(jnp.where((order > place) & (start_all > 0.5), order, devices))

    def total(pick, values):
        return jnp.sum(jnp.where(pick[:, None, None, None], values, 0.0), axis=0)

    before = total((order < place) & (order >= last_start), kv_all)
    after = total((order > place) & (order <= next_start), qg_all)

    def body(inputs, outs, scratch):
        q, k, v, g, inner_kv, inner_qg, scale, first, a, dq, dk, dv, kv_ref, qg_ref = inputs
        made = make_pairs(scratch, 2)
        zero = jnp.int32(0)
        for p in (
            Pair(True, zero, (q, g), inner_kv, (scale, first), (a, dq), kv_ref, made[0][1], outs[:2], made[0][2]),
            Pair(False, zero, (v, k), inner_qg, (scale, first), (dk, dv), qg_ref, made[1][1], outs[2:], made[1][2]),
        ):
            p.run()
            p.wait()

    return tuple(final(body, (*arrays, *inner, *layout, *parts, before, after), (count, width), width, 2))


def per_device(query_rows, key_rows, value_rows, grad_out, doc_lengths):
    *arrays, doc_lengths = (
        pltpu.with_memory_space_constraint(a, pltpu.HBM)
        for a in (query_rows, key_rows, value_rows, grad_out, doc_lengths)
    )
    if lax.axis_size("seq") == 8:
        return on_eight(arrays, doc_lengths)
    return on_any(arrays, doc_lengths)


def solution(mesh):
    placed = P("seq", "head")
    return jax.shard_map(
        per_device,
        mesh=mesh,
        in_specs=(placed, placed, placed, placed, P()),
        out_specs=(placed, placed, placed, placed),
        check_vma=False,
    )
```
